128 devices in a mesh: bx: 16 (over x, z), by: 8 (over y, core).
Axes of the slice: x: 4, y: 4, z: 4, core: 2. Of those that a mesh axis runs over, the one named last changes fastest.
Arguments:
- features: bfloat16 [16, 8, 1024, 128], P('bx', 'by'), may hold values from -13 to 13
- live_count: int32 [16, 8], P('bx', 'by'), may hold values from 128 to 1024, as said below
- neighbour_map: int32 [16, 8, 27, 1024], P('bx', 'by'), may hold values from 0 to 2175, as said below
- send_rows: int32 [16, 8, 8, 128], P('bx', 'by'), may hold values from 0 to 1023, as said below
- weight: bfloat16 [3456, 128], replicated, may hold values from -0.109375 to 0.109375
- gain: float32 [128], replicated, may hold values from 0.5 to 1.5
- shift: float32 [128], replicated, may hold values from -3 to 3
- cotangent: bfloat16 [16, 8, 1024, 128], P('bx', 'by'), may hold values from -13 to 13
Outputs:
- activated: bfloat16 [16, 8, 1024, 128], P('bx', 'by')
- grad_features: bfloat16 [16, 8, 1024, 128], P('bx', 'by')
- grad_weight: float32 [27, 128, 128], P(None, 'bx', 'by')
The draws below stay inside these ranges and needn't reach their ends.
Inputs may be any that keep to these rules, and one draw needn't show every extreme that they name: Rows 0 to live_count - 1 of a brick are live, the rest padding; in every draw some brick is full. `send_rows`: every entry is below its brick's live count; the eight blocks follow the directions (dx, dy) in row-major order with the brick's own position left out. `neighbour_map`: entries index the brick's extended table; offset 13 of a live row names that row itself; every entry of a padding row is 1536. With B = min(1024, 512) and q = r // B for a live row r, an entry below 1024 lies in rows q B to q B + B - 1, and an entry 1024 + b * 128 + h of incoming block b other than 4 has h in q * 128 B / 1024 to (q + 1) * 128 B / 1024 - 1.
All inputs are finite; a program needn't handle non-finite values.
Results may differ from the reference program's by a relative error of at most 0.029.
The reference program's roundings to bfloat16 on the way (of `outgoing`, `incoming`, `extended`, `conv_out`, `conv_grad`, `halo_grad` and `returned`) count: a program that leaves them out, or rounds other values in their place, can miss the bound.
Values may be sent and summed in bfloat16 or wider, within the bound.
No kernel may reach another device: no remote copies, remote signals or barrier semaphores. Data moves between devices by JAX's collectives and lax.ppermute only.
A program may use at most 64 MiB of HBM per device.

```python
import jax
import jax.numpy as jnp
from jax import lax

C = 128
OFFSETS = 27
ROWS = 1024
HALO = 128
BRICKS_X = 16
BRICKS_Y = 8


def brick_counts(key):
    bricks = BRICKS_X * BRICKS_Y
    levels = jax.random.randint(jax.random.fold_in(key, 11), (bricks,), 0, 1024)
    spread = ROWS - ROWS // 8
    counts = ROWS // 8 + spread * (levels * levels // 1024) // 1023
    fullest = jax.random.randint(jax.random.fold_in(key, 12), (), 0, bricks)
    counts = jnp.where(jnp.arange(bricks) == fullest, ROWS, counts)
    return counts.reshape(BRICKS_X, BRICKS_Y).astype(jnp.int32)


def draw_live_count(key, part):
    return brick_counts(key)


def draw_send_rows(key, part):
    counts = brick_counts(key)[:, :, None, None]
    return jax.random.randint(jax.random.fold_in(key, 21), (BRICKS_X, BRICKS_Y, 8, HALO), 0, counts).astype(jnp.int32)


def draw_neighbour_map(key, part):
    counts = brick_counts(key)[:, :, None, None]
    shape = (BRICKS_X, BRICKS_Y, OFFSETS, ROWS)
    block_rows = min(ROWS, 512)
    halo_window = HALO // (ROWS // block_rows)
    row_ids = jnp.arange(ROWS, dtype=jnp.int32)[None, None, None, :]
    block_index = row_ids // block_rows
    start = block_index * block_rows
    room = jnp.maximum(jnp.minimum(block_rows, counts - start), 1)
    kinds = jax.random.randint(jax.random.fold_in(key, 31), shape, 0, 8)
    local = start + jax.random.randint(jax.random.fold_in(key, 32), shape, 0, room)
    slot = jax.random.randint(jax.random.fold_in(key, 33), shape, 0, 8)
    target = slot + (slot >= 4).astype(jnp.int32)
    remote = ROWS + target * HALO + block_index * halo_window + jax.random.randint(jax.random.fold_in(key, 34), shape, 0, halo_window)
    absent = ROWS + 4 * HALO
    chosen = jnp.where(kinds < 3, absent, jnp.where(kinds < 6, local, remote))
    offset_ids = jnp.arange(OFFSETS, dtype=jnp.int32)[None, None, :, None]
    chosen = jnp.where(offset_ids == 13, row_ids, chosen)
    chosen = jnp.where(row_ids < counts, chosen, absent)
    return chosen.astype(jnp.int32)


def rising_field(key):
    shape = (BRICKS_X, BRICKS_Y, ROWS, C)
    position = (jnp.arange(BRICKS_X)[:, None] * BRICKS_Y + jnp.arange(BRICKS_Y)[None, :]).astype(jnp.float32)
    rise = 1.0 + 2.0 * position / max(BRICKS_X * BRICKS_Y - 1, 1)
    base = jax.random.truncated_normal(jax.random.fold_in(key, 41), -4.0, 4.0, shape, jnp.float32)
    offsets = jax.random.uniform(jax.random.fold_in(key, 42), (C,), jnp.float32, -1.0, 1.0)
    return (base * rise[:, :, None, None] + offsets).astype(jnp.bfloat16)


def draw_features(key, part):
    return rising_field(jax.random.fold_in(key, 51))


def draw_cotangent(key, part):
    return rising_field(jax.random.fold_in(key, 52))


def normal_values(key, dims, scale, bound, kind=jnp.bfloat16):
    return jnp.clip(scale * jax.random.normal(key, dims, jnp.float32), -bound, bound).astype(kind)


def setup_inputs(seed: int = 0) -> dict:
    splits = jax.random.split(jax.random.key(seed), 9)
    features = draw_features(jax.random.fold_in(splits[8], 71), 0)
    live_count = draw_live_count(jax.random.fold_in(splits[8], 71), 0)
    neighbour_map = draw_neighbour_map(jax.random.fold_in(splits[8], 71), 0)
    send_rows = draw_send_rows(jax.random.fold_in(splits[8], 71), 0)
    weight = normal_values(splits[4], (OFFSETS * C, C), (OFFSETS * C) ** -0.5, 0.109375)
    gain = jnp.clip(1.0 + 0.1 * jax.random.normal(splits[5], (C,), jnp.float32), 0.5, 1.5)
    shift = normal_values(splits[6], (C,), 0.5, 3.0, jnp.float32)
    cotangent = draw_cotangent(jax.random.fold_in(splits[8], 71), 0)
    return {"features": features, "live_count": live_count, "neighbour_map": neighbour_map, "send_rows": send_rows, "weight": weight, "gain": gain, "shift": shift, "cotangent": cotangent}


def incoming_blocks(blocks):
    padded = jnp.pad(blocks, ((1, 1), (1, 1), (0, 0), (0, 0), (0, 0)))
    parts = []
    for place in range(9):
        first = place // 3
        second = place % 3
        parts.append(padded[first:first + BRICKS_X, second:second + BRICKS_Y, 8 - place])
    return jnp.stack(parts, axis=2)

def reference(features, live_count, neighbour_map, send_rows, weight, gain, shift, cotangent):
    bricks = BRICKS_X * BRICKS_Y
    picked = jax.vmap(jax.vmap(lambda rows, index: rows[index.reshape(-1)]))(features, send_rows)
    picked = picked.reshape(BRICKS_X, BRICKS_Y, 8, HALO, C)
    empty = jnp.zeros((BRICKS_X, BRICKS_Y, 1, HALO, C), jnp.bfloat16)
    outgoing = jnp.concatenate([picked[:, :, :4], empty, picked[:, :, 4:]], axis=2)
    incoming = incoming_blocks(outgoing).reshape(BRICKS_X, BRICKS_Y, 9 * HALO, C)
    extended = jnp.concatenate([features, incoming], axis=2).reshape(bricks, ROWS + 9 * HALO, C)
    maps = neighbour_map.reshape(bricks, OFFSETS, ROWS)

    def forward_one(pair):
        table, indices = pair
        columns = table[indices.T.reshape(-1)].reshape(ROWS, OFFSETS * C)
        return jnp.dot(columns, weight, preferred_element_type=jnp.float32).astype(jnp.bfloat16)
    conv_out = lax.map(forward_one, (extended, maps))
    conv_float = conv_out.astype(jnp.float32)
    row_ids = jnp.arange(ROWS, dtype=jnp.int32)
    live = (row_ids[None, :] < live_count.reshape(bricks, 1)).astype(jnp.float32)[:, :, None]
    total = jnp.sum(live_count.astype(jnp.float32))
    center = lax.optimization_barrier(jnp.sum(conv_float * live, axis=(0, 1))) / total
    deviation = (conv_float - center) * live
    variance = lax.optimization_barrier(jnp.sum(deviation * deviation, axis=(0, 1))) / total
    inverse_std = lax.rsqrt(variance + 1e-05)
    normalized = (conv_float - center) * inverse_std
    before = gain * normalized + shift
    activated = (jnp.maximum(before, 0.0) * live).astype(jnp.bfloat16)
    upstream = cotangent.reshape(bricks, ROWS, C).astype(jnp.float32) * (before > 0.0) * live
    sum_up = lax.optimization_barrier(jnp.sum(upstream, axis=(0, 1)))
    sum_cross = lax.optimization_barrier(jnp.sum(upstream * normalized, axis=(0, 1)))
    conv_grad = (gain * inverse_std * (upstream - live * (sum_up + normalized * sum_cross) / total)).astype(jnp.bfloat16)

    def backward_one(weight_acc, triple):
        table, indices, grad_rows = triple
        columns = table[indices.T.reshape(-1)].reshape(ROWS, OFFSETS * C)
        weight_acc = weight_acc + jnp.dot(columns.T, grad_rows, preferred_element_type=jnp.float32)
        column_grad = jnp.dot(grad_rows, weight.T, preferred_element_type=jnp.float32)
        table_grad = jnp.zeros((ROWS + 9 * HALO, C), jnp.float32).at[indices.T.reshape(-1)].add(column_grad.reshape(-1, C))
        return (weight_acc, table_grad)
    weight_sum, table_grads = lax.scan(backward_one, jnp.zeros((OFFSETS * C, C), jnp.float32), (extended, maps, conv_grad))
    grad_weight = (weight_sum / jnp.sqrt(total)).reshape(OFFSETS, C, C)
    halo_grad = table_grads[:, ROWS:].astype(jnp.bfloat16).reshape(BRICKS_X, BRICKS_Y, 9, HALO, C)
    returned = incoming_blocks(halo_grad)
    slots = jnp.concatenate([returned[:, :, :4], returned[:, :, 5:]], axis=2).reshape(BRICKS_X, BRICKS_Y, 8 * HALO, C).astype(jnp.float32)
    own_grad = table_grads[:, :ROWS].reshape(BRICKS_X, BRICKS_Y, ROWS, C)
    own_grad = jax.vmap(jax.vmap(lambda grads, index, added: grads.at[index.reshape(-1)].add(added)))(own_grad, send_rows, slots)
    return (activated.reshape(BRICKS_X, BRICKS_Y, ROWS, C), own_grad.astype(jnp.bfloat16), grad_weight)
```

```python
import jax
import jax.numpy as jnp
from jax import lax
from jax.sharding import PartitionSpec as P

epsilon = 1e-05
axes = ("bx", "by")


def extended(cells, sides, width):
    for axis, dim in sides:
        count = lax.axis_size(axis)
        ends = count - 1
        head = lax.slice_in_dim(cells, 0, width, axis=dim)
        tail = lax.slice_in_dim(cells, cells.shape[dim] - width, cells.shape[dim], axis=dim)
        cells = jnp.concatenate(
            [
                lax.ppermute(tail, axis, [(i, (i + 1) % count) for i in range(ends)]),
                cells,
                lax.ppermute(head, axis, [((i + 1) % count, i) for i in range(ends)]),
            ],
            axis=dim,
        )
    return cells


def from_neighbours(outgoing):
    padded = extended(outgoing, (("bx", 0), ("by", 1)), 1)
    return padded[::2, ::2]


def everyones(rows):
    devices = lax.axis_size("bx") * lax.axis_size("by")
    copies = jnp.broadcast_to(rows[None], (devices,) + rows.shape)
    return lax.all_to_all(copies, axes, 0, 0, tiled=True)


def per_device(features, live_count, neighbour_map, send_rows, weight, gain, shift, cotangent):
    own_rows = features[0, 0]
    rows_total, channels = own_rows.shape
    halo_rows = send_rows.shape[3]
    block_rows = min(rows_total, 512)
    blocks_count = rows_total // block_rows
    halo_window = halo_rows // blocks_count
    window_rows = block_rows + 8 * halo_window
    bx, by = lax.axis_size("bx"), lax.axis_size("by")
    sent_index = send_rows[0, 0].reshape(-1)
    send_select = (
        sent_index[:, None] == lax.broadcasted_iota(jnp.int32, (1, rows_total), 1)
    ).astype(jnp.bfloat16)
    chosen_rows = jnp.dot(send_select, own_rows, preferred_element_type=jnp.float32).astype(
        jnp.bfloat16
    )
    chosen_rows = chosen_rows.reshape(8, halo_rows, channels)
    blank_block = jnp.zeros((1, halo_rows, channels), jnp.bfloat16)
    outgoing = jnp.concatenate([chosen_rows[:4], blank_block, chosen_rows[4:]], axis=0).reshape(
        3, 3, halo_rows, channels
    )
    incoming = from_neighbours(outgoing).reshape(9, halo_rows, channels)
    incoming = jnp.concatenate([incoming[:4], incoming[5:]], axis=0).reshape(
        8, blocks_count, halo_window, channels
    )
    index_blocks = neighbour_map[0, 0].reshape(27, blocks_count, block_rows).transpose(1, 0, 2)
    own_blocks = own_rows.reshape(blocks_count, block_rows, channels)
    halo_blocks = incoming.transpose(1, 0, 2, 3)
    block_ids = jnp.arange(blocks_count, dtype=jnp.int32)

    def selector_of(indices, block_index):
        beyond = indices - rows_total
        target = beyond // halo_rows
        inside = beyond - target * halo_rows - block_index * halo_window
        local_pos = indices - block_index * block_rows
        slot = target - (target > 4)
        remote_pos = block_rows + slot * halo_window + inside
        usable = (inside >= 0) & (inside < halo_window) & (target != 4)
        position = jnp.where(indices < rows_total, local_pos, jnp.where(usable, remote_pos, -1))
        return position[:, :, None] == lax.broadcasted_iota(jnp.int32, (1, 1, window_rows), 2)

    def forward_block(pieces):
        indices, own_part, halo_part, block_index = pieces
        window = jnp.concatenate([own_part, halo_part.reshape(8 * halo_window, channels)], axis=0)
        selector = selector_of(indices, block_index).astype(jnp.bfloat16)
        gathered = jnp.einsum(
            "kbw,wc->bkc", selector, window, preferred_element_type=jnp.float32
        ).astype(jnp.bfloat16)
        columns = gathered.reshape(block_rows, 27 * channels)
        return (jnp.dot(columns, weight, preferred_element_type=jnp.float32), columns)

    conv_blocks, column_blocks = lax.map(
        forward_block, (index_blocks, own_blocks, halo_blocks, block_ids)
    )
    conv_out = conv_blocks.reshape(rows_total, channels).astype(jnp.bfloat16)
    conv_float = conv_out.astype(jnp.float32)
    live_mask = (lax.broadcasted_iota(jnp.int32, (rows_total, 1), 0) < live_count[0, 0]).astype(
        jnp.float32
    )
    local_count = live_count[0, 0].astype(jnp.float32)
    local_mean = jnp.sum(conv_float * live_mask, axis=0) / local_count
    local_dev = (conv_float - local_mean) * live_mask
    local_square = jnp.sum(local_dev * local_dev, axis=0)
    stats = everyones(
        jnp.stack([local_mean, local_square, jnp.full((channels,), local_count)])
    ).reshape(bx * by, 3, channels)
    counts = stats[:, 2]
    total_count = jnp.sum(counts, axis=0)
    center = jnp.sum(stats[:, 0] * counts, axis=0) / total_count
    apart = stats[:, 0] - center
    variance = jnp.sum(stats[:, 1] + counts * apart * apart, axis=0) / total_count
    inverse_std = lax.rsqrt(variance + epsilon)
    normalized = (conv_float - center) * inverse_std
    before = gain * normalized + shift
    activated = (jnp.maximum(before, 0.0) * live_mask).astype(jnp.bfloat16)
    upstream = cotangent[0, 0].astype(jnp.float32) * (before > 0.0) * live_mask
    sums = everyones(
        jnp.stack([jnp.sum(upstream, axis=0), jnp.sum(upstream * normalized, axis=0)])
    ).reshape(bx * by, 2, channels)
    sum_up, sum_cross = jnp.sum(sums[:, 0], axis=0), jnp.sum(sums[:, 1], axis=0)
    conv_grad = (
        gain
        * inverse_std
        * (upstream - live_mask * (sum_up + normalized * sum_cross) / total_count)
    ).astype(jnp.bfloat16)
    grad_blocks = conv_grad.reshape(blocks_count, block_rows, channels)

    def backward_block(weight_acc, pieces):
        indices, columns, grad_rows, block_index = pieces
        weight_acc = weight_acc + lax.dot_general(
            columns, grad_rows, (((0,), (0,)), ((), ())), preferred_element_type=jnp.float32
        )
        column_grad = lax.dot_general(
            grad_rows, weight, (((1,), (1,)), ((), ())), preferred_element_type=jnp.float32
        ).astype(jnp.bfloat16)
        column_grad = column_grad.reshape(block_rows, 27, channels)
        selector = selector_of(indices, block_index).astype(jnp.bfloat16)
        window_grad = jnp.einsum(
            "kbw,bkc->wc",
            selector,
            column_grad,
            preferred_element_type=jnp.float32,
        )
        return (
            weight_acc,
            (window_grad[:block_rows], window_grad[block_rows:].reshape(8, halo_window, channels)),
        )

    start_acc = jnp.zeros((27 * channels, channels), jnp.float32)
    weight_acc, (own_parts, halo_parts) = lax.scan(
        backward_block, start_acc, (index_blocks, column_blocks, grad_blocks, block_ids)
    )
    weight_terms = weight_acc.astype(jnp.bfloat16).reshape(
        27, bx, channels // bx, by, channels // by
    )
    pieces = weight_terms.transpose(1, 3, 0, 2, 4).reshape(bx * by, 27, channels)
    pieces = jnp.pad(pieces, ((0, 0), (0, 5), (0, 0)))
    arrived = lax.all_to_all(pieces, axes, 0, 0, tiled=True)
    summed = jnp.sum(arrived[:, :27].astype(jnp.float32), axis=0)
    grad_weight = summed.reshape(27, channels // bx, channels // by) / jnp.sqrt(total_count[0])
    own_table = own_parts.reshape(rows_total, channels)
    halo_table = halo_parts.transpose(1, 0, 2, 3).reshape(8, halo_rows, channels)
    halo_grad = halo_table.astype(jnp.bfloat16)
    halo_grad = jnp.concatenate([halo_grad[:4], blank_block, halo_grad[4:]], axis=0).reshape(
        3, 3, halo_rows, channels
    )
    returned = from_neighbours(halo_grad).reshape(9, halo_rows, channels)
    slots_back = jnp.concatenate([returned[:4], returned[5:]], axis=0).reshape(-1, channels)
    added_back = lax.dot_general(
        send_select,
        slots_back,
        (((0,), (0,)), ((), ())),
        preferred_element_type=jnp.float32,
    )
    own_grad = own_table + added_back
    return (activated[None, None], own_grad.astype(jnp.bfloat16)[None, None], grad_weight)


def solution(mesh):
    return jax.shard_map(
        per_device,
        mesh=mesh,
        in_specs=(
            P("bx", "by", None, None),
            P("bx", "by"),
            P("bx", "by", None, None),
            P("bx", "by", None, None),
            P(),
            P(),
            P(),
            P("bx", "by", None, None),
        ),
        out_specs=(P("bx", "by", None, None), P("bx", "by", None, None), P(None, "bx", "by")),
        check_vma=False,
    )
```

```python
import functools

import jax
import jax.numpy as jnp
from jax import lax
from jax.experimental import pallas as pl
from jax.experimental.pallas import tpu as pltpu
from jax.sharding import PartitionSpec as P

epsilon = 1e-05
axes = ("bx", "by")
F32, BF16, I32 = jnp.float32, jnp.bfloat16, jnp.int32
TAPS = 27


def forward_kernel(tile, place_ref, own_ref, a0_ref, a2_ref, b0_ref, b2_ref, weight_ref, conv_ref, cols_ref, win_ref):
    rows, channels = own_ref.shape
    block = win_ref.shape[0]
    part = block // 8
    high = a0_ref.shape[0] // 3
    for q in range(rows // block):
        win_ref[:, :channels] = own_ref[pl.ds(q * block, block), :]
        pieces = (
            (b0_ref, 0), (a0_ref, 1), (b2_ref, 0), (b0_ref, 1),
            (b2_ref, 1), (b0_ref, 2), (a2_ref, 1), (b2_ref, 2),
        )
        for slot, (ref, at) in enumerate(pieces):
            win_ref[pl.ds(slot * part, part), channels:] = ref[pl.ds(at * high + q * part, part), :]
        lanes = lax.broadcasted_iota(I32, (tile, block), 1)

        def rows_step(t, _):
            start = pl.multiple_of(q * block + t * tile, tile)
            place = place_ref[pl.ds(start, tile), :]
            for k in range(TAPS):
                column = jnp.broadcast_to(place[:, k : k + 1], (tile, channels))
                beyond = column >= block
                inside = jnp.where(beyond, column - block, column)
                hot = jnp.concatenate(
                    [
                        jnp.where(inside == lanes[:, c : c + channels], 1.0, 0.0).astype(BF16)
                        for c in range(0, block, channels)
                    ],
                    axis=1,
                )
                both = jnp.dot(hot, win_ref[...], preferred_element_type=F32)
                cols_ref[pl.ds(start, tile), k * channels : (k + 1) * channels] = jnp.where(
                    beyond, both[:, channels:], both[:, :channels]
                ).astype(BF16)
            conv_ref[pl.ds(start, tile), :] = jnp.dot(
                cols_ref[pl.ds(start, tile), :], weight_ref[...], preferred_element_type=F32
            ).astype(BF16)
            return 0

        lax.fori_loop(0, block // tile, rows_step, 0)


def forward(place, own, a0, a2, b0, b2, weight, block=512, tile=512):
    rows, channels = own.shape
    return pl.pallas_call(
        functools.partial(forward_kernel, tile),
        out_shape=(
            jax.ShapeDtypeStruct((rows, channels), BF16),
            jax.ShapeDtypeStruct((rows, TAPS * channels), BF16),
        ),
        scratch_shapes=[pltpu.VMEM((block, 2 * channels), BF16)],
        compiler_params=pltpu.CompilerParams(vmem_limit_bytes=40 << 20),
    )(place, own, a0, a2, b0, b2, weight)


def backward_kernel(group, row_ref, place_ref, grad_ref, weight_ref, own_ref, lo_ref, m0_ref, m2_ref, hi_ref, acc_ref, hot_ref, rhs_ref):
    rows, channels = grad_ref.shape
    block = acc_ref.shape[0]
    part = block // 8
    high = m0_ref.shape[0]
    for q in range(rows // block):
        grad = grad_ref[pl.ds(q * block, block), :]
        place = place_ref[pl.ds(q * block, block), :]
        down = lax.broadcasted_iota(I32, (block, block), 0)
        for g in range(TAPS // group):
            for n in range(group):
                k = g * group + n
                line = row_ref[k : k + 1, pl.ds(q * block, block)]
                line = jnp.where(line >= block, line - block, line)
                hot_ref[:, n * block : (n + 1) * block] = jnp.where(
                    jnp.broadcast_to(line, (block, block)) == down, 1.0, 0.0
                ).astype(BF16)
                back = lax.dot_general(
                    grad, weight_ref[k * channels : (k + 1) * channels, :],
                    (((1,), (1,)), ((), ())), preferred_element_type=F32,
                )
                beyond = jnp.broadcast_to(place[:, k : k + 1], (block, channels)) >= block
                rhs_ref[n * block : (n + 1) * block, :channels] = jnp.where(beyond, 0.0, back).astype(BF16)
                rhs_ref[n * block : (n + 1) * block, channels:] = jnp.where(beyond, back, 0.0).astype(BF16)
            term = jnp.dot(hot_ref[...], rhs_ref[...], preferred_element_type=F32)
            if g == 0:
                acc_ref[...] = term
            else:
                acc_ref[...] += term
        own_ref[pl.ds(q * block, block), :] = acc_ref[:, :channels]
        pieces = (
            (lo_ref, 0), (lo_ref, 1), (lo_ref, 2), (m0_ref, 0),
            (m2_ref, 0), (hi_ref, 0), (hi_ref, 1), (hi_ref, 2),
        )
        for slot, (ref, at) in enumerate(pieces):
            ref[pl.ds(at * high + q * part, part), :] = acc_ref[slot * part : (slot + 1) * part, channels:].astype(BF16)


def backward(row, place, grad, weight, high, block=512, group=3):
    rows, channels = grad.shape
    return pl.pallas_call(
        functools.partial(backward_kernel, group),
        out_shape=(
            jax.ShapeDtypeStruct((rows, channels), F32),
            jax.ShapeDtypeStruct((3 * high, channels), BF16),
            jax.ShapeDtypeStruct((high, channels), BF16),
            jax.ShapeDtypeStruct((high, channels), BF16),
            jax.ShapeDtypeStruct((3 * high, channels), BF16),
        ),
        scratch_shapes=[
            pltpu.VMEM((block, 2 * channels), F32),
            pltpu.VMEM((block, group * block), BF16),
            pltpu.VMEM((group * block, 2 * channels), BF16),
        ],
        compiler_params=pltpu.CompilerParams(vmem_limit_bytes=40 << 20),
    )(row, place, grad, weight)


def terms_kernel(across, down, cols_ref, rhs_ref, *outs):
    channels = cols_ref.shape[1] // TAPS
    width = channels // down
    sub = lax.broadcasted_iota(I32, (across, down, channels), 1)
    lane = lax.broadcasted_iota(I32, (across, down, channels), 2)

    for k in range(TAPS):
        whole = lax.dot_general(
            cols_ref[:, k * channels : (k + 1) * channels], rhs_ref[...],
            (((0,), (0,)), ((), ())), preferred_element_type=F32,
        )
        for n, out_ref in enumerate(outs):
            tiles = whole[:, n * channels : (n + 1) * channels].reshape(across, down, channels)
            step = 1
            while step < down:
                shift = step * width
                high_row = (sub & step) != 0
                high_lane = (lane & shift) != 0
                from_below = pltpu.roll(pltpu.roll(tiles, shift, 2), down - step, 1)
                from_above = pltpu.roll(pltpu.roll(tiles, channels - shift, 2), step, 1)
                tiles = jnp.where(
                    high_row == high_lane, tiles, jnp.where(high_row, from_above, from_below)
                )
                step *= 2
            out_ref[:, k, :] = tiles.reshape(across * down, channels)
    for out_ref in outs:
        for k in range(TAPS, out_ref.shape[1]):
            out_ref[:, k, :] = jnp.zeros((across * down, channels), F32)


def weight_parts(cols, rhs, across, down, count):
    rows, wide = cols.shape
    channels = wide // TAPS
    return pl.pallas_call(
        functools.partial(terms_kernel, across, down),
        out_shape=tuple(
            jax.ShapeDtypeStruct((across * down, 32, channels), F32) for _ in range(count)
        ),
        compiler_params=pltpu.CompilerParams(vmem_limit_bytes=40 << 20),
        cost_estimate=pl.CostEstimate(
            flops=2 * rows * wide * channels * count, bytes_accessed=10 << 20, transcendentals=0
        ),
    )(cols, rhs)


def combine_kernel(down, first_ref, second_ref, third_ref, scale_ref, out_ref):
    devices, taps, channels = out_ref.shape
    width = channels // down
    row = lax.broadcasted_iota(I32, (down, channels), 0)
    lane = lax.broadcasted_iota(I32, (down, channels), 1)
    spread = jnp.where(
        lax.broadcasted_iota(I32, (channels, channels), 0) % width
        == lax.broadcasted_iota(I32, (channels, channels), 1) % width,
        1.0,
        0.0,
    )

    def placed(n):
        own = jnp.where(lane // width == row, jnp.broadcast_to(scale_ref[n : n + 1, :], (down, channels)), 0.0)
        return jnp.dot(own, spread, precision=lax.Precision.HIGHEST, preferred_element_type=F32)

    scales = [placed(n) for n in range(3)]
    for d in range(devices):
        y = d % down
        out_ref[d] = (
            first_ref[d] * scales[0][y : y + 1]
            - second_ref[d] * scales[1][y : y + 1]
            - third_ref[d] * scales[2][y : y + 1]
        ).astype(BF16)


def combine(first, second, third, scales, down):
    return pl.pallas_call(
        functools.partial(combine_kernel, down),
        out_shape=jax.ShapeDtypeStruct(first.shape, BF16),
        compiler_params=pltpu.CompilerParams(vmem_limit_bytes=40 << 20),
        cost_estimate=pl.CostEstimate(flops=5 << 19, bytes_accessed=7 << 20, transcendentals=0),
    )(first, second, third, scales)


def from_neighbours(low, mid_low, mid_high, high):
    size = mid_low.shape[0]
    ends_x, ends_y = lax.axis_size("bx") - 1, lax.axis_size("by") - 1
    up_x, down_x = [(i, i + 1) for i in range(ends_x)], [(i + 1, i) for i in range(ends_x)]
    up_y, down_y = [(i, i + 1) for i in range(ends_y)], [(i + 1, i) for i in range(ends_y)]
    a0 = lax.ppermute(high, "bx", up_x)
    a2 = lax.ppermute(low, "bx", down_x)
    b0 = lax.ppermute(jnp.concatenate([a0[2 * size :], mid_high, a2[2 * size :]]), "by", up_y)
    b2 = lax.ppermute(jnp.concatenate([a0[:size], mid_low, a2[:size]]), "by", down_y)
    return a0, a2, b0, b2


def everyones(rows):
    devices = lax.axis_size("bx") * lax.axis_size("by")
    copies = jnp.broadcast_to(rows[None], (devices,) + rows.shape)
    return lax.all_to_all(copies, axes, 0, 0, tiled=True)


def per_device(features, live_count, neighbour_map, send_rows, weight, gain, shift, cotangent):
    own_rows = features[0, 0]
    rows_total, channels = own_rows.shape
    size = send_rows.shape[3]
    block_rows = min(rows_total, 512)
    part = size * block_rows // rows_total
    across, down = lax.axis_size("bx"), lax.axis_size("by")
    sent_index = send_rows[0, 0].reshape(-1)
    send_select = (
        sent_index[:, None] == lax.broadcasted_iota(I32, (1, rows_total), 1)
    ).astype(BF16)
    chosen = jnp.dot(send_select, own_rows, preferred_element_type=F32).astype(BF16)
    a0, a2, b0, b2 = from_neighbours(
        chosen[: 3 * size], chosen[3 * size : 4 * size], chosen[4 * size : 5 * size], chosen[5 * size :]
    )

    indices = neighbour_map[0, 0]
    block = lax.broadcasted_iota(I32, (1, rows_total), 1) // block_rows
    beyond = indices - rows_total
    target = beyond // size
    inside = beyond - target * size - block * part
    remote = block_rows + (target - (target > 4)) * part + inside
    usable = (inside >= 0) & (inside < part) & (target != 4)
    place = jnp.where(
        indices < rows_total, indices - block * block_rows, jnp.where(usable, remote, -1)
    )
    place = jnp.pad(place, ((0, 5), (0, 0)), constant_values=-1)
    place_down = place.T

    conv_out, cols = forward(place_down, own_rows, a0, a2, b0, b2, weight)
    conv_float = conv_out.astype(F32)
    live_mask = (lax.broadcasted_iota(I32, (rows_total, 1), 0) < live_count[0, 0]).astype(F32)
    local_count = live_count[0, 0].astype(F32)
    local_mean = jnp.sum(conv_float * live_mask, axis=0) / local_count
    local_dev = (conv_float - local_mean) * live_mask
    local_square = jnp.sum(local_dev * local_dev, axis=0)
    stats = everyones(
        jnp.stack([local_mean, local_square, jnp.full((channels,), local_count)])
    )
    both = jnp.concatenate(
        [jnp.broadcast_to(live_mask, (rows_total, channels)).astype(BF16), conv_out], axis=1
    )
    ones_part, conv_part = weight_parts(cols, both, across, down, 2)
    counts = stats[:, 2]
    total_count = jnp.sum(counts, axis=0)
    center = jnp.sum(stats[:, 0] * counts, axis=0) / total_count
    apart = stats[:, 0] - center
    variance = jnp.sum(stats[:, 1] + counts * apart * apart, axis=0) / total_count
    inverse_std = lax.rsqrt(variance + epsilon)
    normalized = (conv_float - center) * inverse_std
    before = gain * normalized + shift
    activated = (jnp.maximum(before, 0.0) * live_mask).astype(BF16)
    upstream = cotangent[0, 0].astype(F32) * (before > 0.0) * live_mask
    sums = everyones(
        jnp.stack([jnp.sum(upstream, axis=0), jnp.sum(upstream * normalized, axis=0)])
    )
    (up_part,) = weight_parts(cols, upstream.astype(BF16), across, down, 1)
    mean_up = jnp.sum(sums[:, 0], axis=0) / total_count
    mean_cross = jnp.sum(sums[:, 1], axis=0) / total_count
    scale = gain * inverse_std
    conv_grad = (
        scale * (upstream - live_mask * (mean_up + normalized * mean_cross))
    ).astype(BF16)

    scales = jnp.stack(
        [
            scale,
            scale * (mean_up - mean_cross * inverse_std * center),
            scale * mean_cross * inverse_std,
        ]
    )
    pieces = combine(up_part, ones_part, conv_part, scales, down)
    arrived = lax.all_to_all(pieces, axes, 0, 0, tiled=True)
    own_table, *halo = backward(place, place_down, conv_grad, weight, size)
    a0, a2, b0, b2 = from_neighbours(*halo)
    slots_back = jnp.concatenate(
        [
            b0[:size], a0[size : 2 * size], b2[:size], b0[size : 2 * size],
            b2[size : 2 * size], b0[2 * size :], a2[size : 2 * size], b2[2 * size :],
        ]
    )
    added_back = lax.dot_general(
        send_select,
        slots_back,
        (((0,), (0,)), ((), ())),
        preferred_element_type=F32,
    )
    own_grad = (own_table + added_back).astype(BF16)
    summed = jnp.sum(arrived[:, :TAPS].astype(F32), axis=0)
    grad_weight = summed.reshape(TAPS, channels // across, channels // down) / jnp.sqrt(
        total_count[0]
    )
    return (activated[None, None], own_grad[None, None], grad_weight)


def solution(mesh):
    return jax.shard_map(
        per_device,
        mesh=mesh,
        in_specs=(
            P("bx", "by", None, None),
            P("bx", "by"),
            P("bx", "by", None, None),
            P("bx", "by", None, None),
            P(),
            P(),
            P(),
            P("bx", "by", None, None),
        ),
        out_specs=(P("bx", "by", None, None), P("bx", "by", None, None), P(None, "bx", "by")),
        check_vma=False,
    )
```

```python
import functools

import jax
import jax.numpy as jnp
from jax import lax
from jax.experimental import pallas as pl
from jax.experimental.pallas import tpu as pltpu
from jax.sharding import PartitionSpec as P

epsilon = 1e-05
axes = ("bx", "by")
F32, BF16, I32 = jnp.float32, jnp.bfloat16, jnp.int32
TAPS = 27


def forward_kernel(chunks, place_ref, own_ref, a0_ref, a2_ref, b0_ref, b2_ref, weight_ref, conv_ref, out_ref, win_ref, cols_ref, sems):
    rows, channels = own_ref.shape
    block = win_ref.shape[0]
    part = block // 8
    high = a0_ref.shape[0] // 3
    wide = TAPS // chunks * channels
    lanes = lax.broadcasted_iota(I32, (block, block), 1)

    def copy_out(q, c):
        return pltpu.make_async_copy(
            cols_ref.at[q, :, pl.ds(c * wide, wide)],
            out_ref.at[pl.ds(q * block, block), pl.ds(c * wide, wide)],
            sems.at[q, c],
        )

    def block_step(q, _):
        here = pl.ds(pl.multiple_of(q * block, block), block)
        win_ref[:, :channels] = own_ref[here, :]
        pieces = (
            (b0_ref, 0), (a0_ref, 1), (b2_ref, 0), (b0_ref, 1),
            (b2_ref, 1), (b0_ref, 2), (a2_ref, 1), (b2_ref, 2),
        )
        for slot, (ref, at) in enumerate(pieces):
            win_ref[pl.ds(slot * part, part), channels:] = ref[
                pl.ds(pl.multiple_of(at * high + q * part, part), part), :
            ]
        place = place_ref[here, :]
        for k in range(TAPS):
            column = jnp.broadcast_to(place[:, k : k + 1], (block, channels))
            beyond = column >= block
            inside = jnp.where(beyond, column - block, column)
            hot = jnp.concatenate(
                [
                    jnp.where(inside == lanes[:, c : c + channels], 1.0, 0.0).astype(BF16)
                    for c in range(0, block, channels)
                ],
                axis=1,
            )
            both = jnp.dot(hot, win_ref[...], preferred_element_type=F32)
            cols_ref[q, :, k * channels : (k + 1) * channels] = jnp.where(
                beyond, both[:, channels:], both[:, :channels]
            ).astype(BF16)
            if (k + 1) % (TAPS // chunks) == 0:
                copy_out(q, k // (TAPS // chunks)).start()
        conv_ref[here, :] = jnp.dot(
            cols_ref[q], weight_ref[...], preferred_element_type=F32
        ).astype(BF16)
        return 0

    lax.fori_loop(0, rows // block, block_step, 0)
    for q in range(rows // block):
        for c in range(chunks):
            copy_out(q, c).wait()


def forward(place, own, a0, a2, b0, b2, weight, block=512, chunks=3):
    rows, channels = own.shape
    vmem = pl.BlockSpec(memory_space=pltpu.VMEM)
    return pl.pallas_call(
        functools.partial(forward_kernel, chunks),
        in_specs=[vmem] * 7,
        out_specs=(vmem, pl.BlockSpec(memory_space=pltpu.HBM)),
        out_shape=(
            jax.ShapeDtypeStruct((rows, channels), BF16),
            pltpu.HBM((rows, TAPS * channels), BF16),
        ),
        scratch_shapes=[
            pltpu.VMEM((block, 2 * channels), BF16),
            pltpu.VMEM((rows // block, block, TAPS * channels), BF16),
            pltpu.SemaphoreType.DMA((rows // block, chunks)),
        ],
        compiler_params=pltpu.CompilerParams(vmem_limit_bytes=20 << 20),
        cost_estimate=pl.CostEstimate(
            flops=TAPS * 4 * rows * channels * block, bytes_accessed=9 << 20, transcendentals=0
        ),
    )(place, own, a0, a2, b0, b2, weight)


def backward_kernel(group, row_ref, place_ref, grad_ref, weight_ref, own_ref, lo_ref, m0_ref, m2_ref, hi_ref, acc_ref, hot_ref, rhs_ref):
    rows, channels = grad_ref.shape
    block = acc_ref.shape[0]
    part = block // 8
    high = m0_ref.shape[0]
    for q in range(rows // block):
        grad = grad_ref[pl.ds(q * block, block), :]
        place = place_ref[pl.ds(q * block, block), :]
        down = lax.broadcasted_iota(I32, (block, block), 0)
        for g in range(TAPS // group):
            for n in range(group):
                k = g * group + n
                line = row_ref[q, k : k + 1, :]
                line = jnp.where(line >= block, line - block, line)
                hot_ref[:, n * block : (n + 1) * block] = jnp.where(
                    jnp.broadcast_to(line, (block, block)) == down, 1.0, 0.0
                ).astype(BF16)
                back = lax.dot_general(
                    grad, weight_ref[k * channels : (k + 1) * channels, :],
                    (((1,), (1,)), ((), ())), preferred_element_type=F32,
                )
                beyond = jnp.broadcast_to(place[:, k : k + 1], (block, channels)) >= block
                rhs_ref[n * block : (n + 1) * block, :channels] = jnp.where(beyond, 0.0, back).astype(BF16)
                rhs_ref[n * block : (n + 1) * block, channels:] = jnp.where(beyond, back, 0.0).astype(BF16)
            term = jnp.dot(hot_ref[...], rhs_ref[...], preferred_element_type=F32)
            if g == 0:
                acc_ref[...] = term
            else:
                acc_ref[...] += term
        own_ref[pl.ds(q * block, block), :] = acc_ref[:, :channels]
        pieces = (
            (lo_ref, 0), (lo_ref, 1), (lo_ref, 2), (m0_ref, 0),
            (m2_ref, 0), (hi_ref, 0), (hi_ref, 1), (hi_ref, 2),
        )
        for slot, (ref, at) in enumerate(pieces):
            ref[pl.ds(at * high + q * part, part), :] = acc_ref[slot * part : (slot + 1) * part, channels:].astype(BF16)


def backward(row, place, grad, weight, high, block=512, group=3):
    rows, channels = grad.shape
    return pl.pallas_call(
        functools.partial(backward_kernel, group),
        out_shape=(
            jax.ShapeDtypeStruct((rows, channels), F32),
            jax.ShapeDtypeStruct((3 * high, channels), BF16),
            jax.ShapeDtypeStruct((high, channels), BF16),
            jax.ShapeDtypeStruct((high, channels), BF16),
            jax.ShapeDtypeStruct((3 * high, channels), BF16),
        ),
        scratch_shapes=[
            pltpu.VMEM((block, 2 * channels), F32),
            pltpu.VMEM((block, group * block), BF16),
            pltpu.VMEM((group * block, 2 * channels), BF16),
        ],
        compiler_params=pltpu.CompilerParams(vmem_limit_bytes=16 << 20),
        cost_estimate=pl.CostEstimate(flops=TAPS*4*rows*channels*(block+64), bytes_accessed=2<<20, transcendentals=0),
    )(row, place, grad, weight)


def terms_kernel(across, down, group, cols_ref, rhs_ref, *refs):
    count = (len(refs) - 4) // 2
    outs, stages = refs[:count], refs[count : 2 * count]
    mirror_ref, buffer_ref, in_sems, out_sems = refs[2 * count :]
    channels = cols_ref.shape[1] // TAPS
    width = channels // down
    slots = buffer_ref.shape[0]
    row = lax.broadcasted_iota(I32, (channels, channels), 0)
    lane = lax.broadcasted_iota(I32, (channels, channels), 1)
    steps = TAPS // group

    def fetch(step):
        return pltpu.make_async_copy(
            cols_ref.at[:, pl.ds(step * group * channels, group * channels)],
            buffer_ref.at[step % slots],
            in_sems.at[step % slots],
        )

    def leave(n, eighth):
        return pltpu.make_async_copy(
            stages[n].at[eighth], outs[n].at[eighth], out_sems.at[n, eighth]
        )

    for step in range(slots - 1):
        fetch(step).start()
    mirror = jnp.where(
        row == (down - lane // width) % down * width + lane % width, 1.0, 0.0
    ).astype(BF16)
    for n in range(count):
        part = slice(n * channels, (n + 1) * channels)
        mirror_ref[:, part] = jnp.dot(
            rhs_ref[:, part], mirror, preferred_element_type=F32
        ).astype(BF16)
    for step in range(steps):
        if step + slots - 1 < steps:
            fetch(step + slots - 1).start()
        fetch(step).wait()
        whole = lax.dot_general(
            buffer_ref[step % slots], mirror_ref[...],
            (((0,), (0,)), ((), ())), preferred_element_type=F32,
        )
        for n in range(count):
            for k in range(step * group, (step + 1) * group):
                at = (k - step * group) * channels
                tile = whole[at : at + channels, n * channels : (n + 1) * channels]
                tile = pltpu.roll(tile, 0, 1, stride=width, stride_axis=0)
                turn = 1
                while turn < down:
                    turned = pltpu.roll(
                        tile.reshape(across, down, channels), down - turn, 1
                    ).reshape(channels, channels)
                    tile = jnp.where((lane & (turn * width)) != 0, turned, tile)
                    turn *= 2
                stages[n][k // 8, :, k % 8, :] = pltpu.roll(
                    tile, 0, 1, stride=width, stride_axis=0
                )
                if k % 8 == 7:
                    leave(n, k // 8).start()
    for n in range(count):
        for k in range(TAPS, 32):
            stages[n][k // 8, :, k % 8, :] = jnp.zeros((channels, channels), F32)
        leave(n, 3).start()
    for n in range(count):
        for eighth in range(4):
            leave(n, eighth).wait()


def weight_parts(cols, rhs, across, down, group=3, slots=3):
    rows, wide = cols.shape
    channels = wide // TAPS
    count = rhs.shape[1] // channels
    hbm = pl.BlockSpec(memory_space=pltpu.HBM)
    shape = (4, across * down, 8, channels)
    return pl.pallas_call(
        functools.partial(terms_kernel, across, down, group),
        in_specs=[hbm, pl.BlockSpec(memory_space=pltpu.VMEM)],
        out_specs=(hbm,) * count,
        out_shape=(pltpu.HBM(shape, F32),) * count,
        scratch_shapes=[pltpu.VMEM(shape, F32)] * count
        + [
            pltpu.VMEM(rhs.shape, BF16),
            pltpu.VMEM((slots, rows, group * channels), BF16),
            pltpu.SemaphoreType.DMA((slots,)),
            pltpu.SemaphoreType.DMA((count, 4)),
        ],
        compiler_params=pltpu.CompilerParams(vmem_limit_bytes=20 << 20),
        cost_estimate=pl.CostEstimate(
            flops=2 * rows * wide * channels * count, bytes_accessed=10 << 20, transcendentals=0
        ),
    )(pltpu.with_memory_space_constraint(cols, pltpu.HBM), rhs)


def combine_kernel(down, first_ref, second_ref, third_ref, scale_ref, out_ref, placed_ref):
    devices, taps, channels = out_ref.shape
    width = channels // down

    @pl.when(pl.program_id(0) == 0)
    def _():
        row = lax.broadcasted_iota(I32, (down, channels), 0)
        lane = lax.broadcasted_iota(I32, (down, channels), 1)
        spread = jnp.where(
            lax.broadcasted_iota(I32, (channels, channels), 0) % width
            == lax.broadcasted_iota(I32, (channels, channels), 1) % width,
            1.0,
            0.0,
        )
        for n in range(3):
            own = jnp.where(
                lane // width == row,
                jnp.broadcast_to(scale_ref[n : n + 1, :], (down, channels)),
                0.0,
            )
            placed_ref[n] = jnp.dot(
                own, spread, precision=lax.Precision.HIGHEST, preferred_element_type=F32
            )

    for d in range(devices):
        y = d % down
        scales = [placed_ref[n, y : y + 1, :] for n in range(3)]
        for e in range(taps // 8):
            out_ref[d, e * 8 : (e + 1) * 8, :] = (
                first_ref[e, d] * scales[0]
                - second_ref[e, d] * scales[1]
                - third_ref[e, d] * scales[2]
            ).astype(BF16)


def combine(first, second, third, scales, down, steps=4):
    eighths, devices, eight, channels = first.shape
    some = devices // steps
    spec = pl.BlockSpec((eighths, some, eight, channels), lambda d: (0, d, 0, 0))
    return pl.pallas_call(
        functools.partial(combine_kernel, down),
        grid=(steps,),
        in_specs=[spec, spec, spec, pl.BlockSpec(scales.shape, lambda d: (0, 0))],
        out_specs=pl.BlockSpec((some, eighths * eight, channels), lambda d: (d, 0, 0)),
        out_shape=jax.ShapeDtypeStruct((devices, eighths * eight, channels), BF16),
        scratch_shapes=[pltpu.VMEM((3, down, channels), F32)],
        compiler_params=pltpu.CompilerParams(vmem_limit_bytes=16 << 20),
        cost_estimate=pl.CostEstimate(flops=5 << 19, bytes_accessed=7 << 20, transcendentals=0),
    )(*(pltpu.with_memory_space_constraint(p, pltpu.HBM) for p in (first, second, third)), scales)


def from_neighbours(low, mid_low, mid_high, high, arrived=None):
    size = mid_low.shape[0]
    ends_x, ends_y = lax.axis_size("bx") - 1, lax.axis_size("by") - 1
    up_x, down_x = [(i, i + 1) for i in range(ends_x)], [(i + 1, i) for i in range(ends_x)]
    up_y, down_y = [(i, i + 1) for i in range(ends_y)], [(i + 1, i) for i in range(ends_y)]
    a0 = lax.ppermute(high, "bx", up_x)
    a2 = lax.ppermute(low, "bx", down_x)
    if arrived is not None:
        a0, a2, arrived = lax.optimization_barrier((a0, a2, arrived))
    b0 = lax.ppermute(jnp.concatenate([a0[2 * size :], mid_high, a2[2 * size :]]), "by", up_y)
    b2 = lax.ppermute(jnp.concatenate([a0[:size], mid_low, a2[:size]]), "by", down_y)
    return a0, a2, b0, b2, arrived


def everyones(rows):
    devices = lax.axis_size("bx") * lax.axis_size("by")
    copies = jnp.broadcast_to(rows[None], (devices,) + rows.shape)
    return lax.all_to_all(copies, axes, 0, 0, tiled=True)


def per_device(features, live_count, neighbour_map, send_rows, weight, gain, shift, cotangent):
    own_rows = features[0, 0]
    rows_total, channels = own_rows.shape
    size = send_rows.shape[3]
    block_rows = min(rows_total, 512)
    part = size * block_rows // rows_total
    across, down = lax.axis_size("bx"), lax.axis_size("by")
    sent_index = send_rows[0, 0].reshape(-1)
    send_select = (
        sent_index[:, None] == lax.broadcasted_iota(I32, (1, rows_total), 1)
    ).astype(BF16)
    chosen = jnp.dot(send_select, own_rows, preferred_element_type=F32).astype(BF16)
    a0, a2, b0, b2, _ = from_neighbours(
        chosen[: 3 * size], chosen[3 * size : 4 * size], chosen[4 * size : 5 * size], chosen[5 * size :]
    )

    indices = neighbour_map[0, 0]
    block = lax.broadcasted_iota(I32, (1, rows_total), 1) // block_rows
    beyond = indices - rows_total
    target = beyond // size
    inside = beyond - target * size - block * part
    remote = block_rows + (target - (target > 4)) * part + inside
    usable = (inside >= 0) & (inside < part) & (target != 4)
    place = jnp.where(
        indices < rows_total, indices - block * block_rows, jnp.where(usable, remote, -1)
    )
    place = jnp.pad(place, ((0, 5), (0, 0)), constant_values=-1)
    place_down = place.T
    place_rows = place.reshape(-1, rows_total // block_rows, block_rows).transpose(1, 0, 2)

    conv_out, cols = forward(place_down, own_rows, a0, a2, b0, b2, weight)
    conv_float = conv_out.astype(F32)
    live_mask = (lax.broadcasted_iota(I32, (rows_total, 1), 0) < live_count[0, 0]).astype(F32)
    local_count = live_count[0, 0].astype(F32)
    local_mean = jnp.sum(conv_float * live_mask, axis=0) / local_count
    local_dev = (conv_float - local_mean) * live_mask
    local_square = jnp.sum(local_dev * local_dev, axis=0)
    stats = everyones(
        jnp.stack([local_mean, local_square, jnp.full((channels,), local_count)])
    )
    both = jnp.concatenate(
        [jnp.broadcast_to(live_mask, (rows_total, channels)).astype(BF16), conv_out], axis=1
    )
    ones_part, conv_part = weight_parts(cols, both, across, down)
    stats, ones_part, conv_part = lax.optimization_barrier((stats, ones_part, conv_part))
    counts = stats[:, 2]
    total_count = jnp.sum(counts, axis=0)
    center = jnp.sum(stats[:, 0] * counts, axis=0) / total_count
    apart = stats[:, 0] - center
    variance = jnp.sum(stats[:, 1] + counts * apart * apart, axis=0) / total_count
    inverse_std = lax.rsqrt(variance + epsilon)
    normalized = (conv_float - center) * inverse_std
    before = gain * normalized + shift
    activated = (jnp.maximum(before, 0.0) * live_mask).astype(BF16)
    upstream = cotangent[0, 0].astype(F32) * (before > 0.0) * live_mask
    sums = everyones(
        jnp.stack([jnp.sum(upstream, axis=0), jnp.sum(upstream * normalized, axis=0)])
    )
    (up_part,) = weight_parts(cols, upstream.astype(BF16), across, down)
    sums, up_part = lax.optimization_barrier((sums, up_part))
    mean_up = jnp.sum(sums[:, 0], axis=0) / total_count
    mean_cross = jnp.sum(sums[:, 1], axis=0) / total_count
    scale = gain * inverse_std
    conv_grad = (
        scale * (upstream - live_mask * (mean_up + normalized * mean_cross))
    ).astype(BF16)

    scales = jnp.stack(
        [
            scale,
            scale * (mean_up - mean_cross * inverse_std * center),
            scale * mean_cross * inverse_std,
        ]
    )
    pieces = combine(up_part, ones_part, conv_part, scales, down)
    pieces, conv_grad = lax.optimization_barrier((pieces, conv_grad))
    arrived = lax.all_to_all(pieces, axes, 0, 0, tiled=True)
    own_table, *halo = backward(place_rows, place_down, conv_grad, weight, size)
    a0, a2, b0, b2, arrived = from_neighbours(*halo, arrived)
    slots_back = jnp.concatenate(
        [
            b0[:size], a0[size : 2 * size], b2[:size], b0[size : 2 * size],
            b2[size : 2 * size], b0[2 * size :], a2[size : 2 * size], b2[2 * size :],
        ]
    )
    added_back = lax.dot_general(
        send_select,
        slots_back,
        (((0,), (0,)), ((), ())),
        preferred_element_type=F32,
    )
    own_grad = (own_table + added_back).astype(BF16)
    summed = jnp.sum(arrived[:, :TAPS].astype(F32), axis=0)
    grad_weight = summed.reshape(TAPS, channels // across, channels // down) / jnp.sqrt(
        total_count[0]
    )
    return (activated[None, None], own_grad[None, None], grad_weight)


def solution(mesh):
    return jax.shard_map(
        per_device,
        mesh=mesh,
        in_specs=(
            P("bx", "by", None, None),
            P("bx", "by"),
            P("bx", "by", None, None),
            P("bx", "by", None, None),
            P(),
            P(),
            P(),
            P("bx", "by", None, None),
        ),
        out_specs=(P("bx", "by", None, None), P("bx", "by", None, None), P(None, "bx", "by")),
        check_vma=False,
    )
```

```python
import functools

import jax
import jax.numpy as jnp
from jax import lax
from jax.experimental import pallas as pl
from jax.experimental.pallas import tpu as pltpu
from jax.sharding import PartitionSpec as P

epsilon = 1e-05
axes = ("bx", "by")
F32, BF16, I32 = jnp.float32, jnp.bfloat16, jnp.int32
TAPS = 27


def forward_kernel(chunks, place_ref, own_ref, a0_ref, a2_ref, b0_ref, b2_ref, weight_ref, conv_ref, out_ref, win_ref, cols_ref, sems):
    rows, channels = own_ref.shape
    block = win_ref.shape[0]
    part = block // 8
    high = a0_ref.shape[0] // 3
    wide = TAPS // chunks * channels
    lanes = lax.broadcasted_iota(I32, (block, block), 1)

    def copy_out(q, c):
        return pltpu.make_async_copy(
            cols_ref.at[q, :, pl.ds(c * wide, wide)],
            out_ref.at[pl.ds(q * block, block), pl.ds(c * wide, wide)],
            sems.at[q, c],
        )

    def block_step(q, _):
        here = pl.ds(pl.multiple_of(q * block, block), block)
        win_ref[:, :channels] = own_ref[here, :]
        pieces = (
            (b0_ref, 0), (a0_ref, 1), (b2_ref, 0), (b0_ref, 1),
            (b2_ref, 1), (b0_ref, 2), (a2_ref, 1), (b2_ref, 2),
        )
        for slot, (ref, at) in enumerate(pieces):
            win_ref[pl.ds(slot * part, part), channels:] = ref[
                pl.ds(pl.multiple_of(at * high + q * part, part), part), :
            ]
        place = place_ref[here, :]
        for k in range(TAPS):
            column = jnp.broadcast_to(place[:, k : k + 1], (block, channels))
            beyond = column >= block
            inside = jnp.where(beyond, column - block, column)
            hot = jnp.concatenate(
                [
                    jnp.where(inside == lanes[:, c : c + channels], 1.0, 0.0).astype(BF16)
                    for c in range(0, block, channels)
                ],
                axis=1,
            )
            both = jnp.dot(hot, win_ref[...], preferred_element_type=F32)
            cols_ref[q, :, k * channels : (k + 1) * channels] = jnp.where(
                beyond, both[:, channels:], both[:, :channels]
            ).astype(BF16)
            if (k + 1) % (TAPS // chunks) == 0:
                copy_out(q, k // (TAPS // chunks)).start()
        conv_ref[here, :] = jnp.dot(
            cols_ref[q], weight_ref[...], preferred_element_type=F32
        ).astype(BF16)
        return 0

    lax.fori_loop(0, rows // block, block_step, 0)
    for q in range(rows // block):
        for c in range(chunks):
            copy_out(q, c).wait()


def forward(place, own, a0, a2, b0, b2, weight, block=512, chunks=3):
    rows, channels = own.shape
    vmem = pl.BlockSpec(memory_space=pltpu.VMEM)
    return pl.pallas_call(
        functools.partial(forward_kernel, chunks),
        in_specs=[vmem] * 7,
        out_specs=(vmem, pl.BlockSpec(memory_space=pltpu.HBM)),
        out_shape=(
            jax.ShapeDtypeStruct((rows, channels), BF16),
            pltpu.HBM((rows, TAPS * channels), BF16),
        ),
        scratch_shapes=[
            pltpu.VMEM((block, 2 * channels), BF16),
            pltpu.VMEM((rows // block, block, TAPS * channels), BF16),
            pltpu.SemaphoreType.DMA((rows // block, chunks)),
        ],
        compiler_params=pltpu.CompilerParams(vmem_limit_bytes=20 << 20),
        cost_estimate=pl.CostEstimate(
            flops=TAPS * 4 * rows * channels * block, bytes_accessed=9 << 20, transcendentals=0
        ),
    )(place, own, a0, a2, b0, b2, weight)


def backward_kernel(group, row_ref, place_ref, grad_ref, weight_ref, own_ref, lo_ref, m0_ref, m2_ref, hi_ref, acc_ref, hot_ref, rhs_ref):
    rows, channels = grad_ref.shape
    block = acc_ref.shape[0]
    part = block // 8
    high = m0_ref.shape[0]
    for q in range(rows // block):
        grad = grad_ref[pl.ds(q * block, block), :]
        place = place_ref[pl.ds(q * block, block), :]
        down = lax.broadcasted_iota(I32, (block, block), 0)
        for g in range(TAPS // group):
            for n in range(group):
                k = g * group + n
                line = row_ref[q, k : k + 1, :]
                line = jnp.where(line >= block, line - block, line)
                hot_ref[:, n * block : (n + 1) * block] = jnp.where(
                    jnp.broadcast_to(line, (block, block)) == down, 1.0, 0.0
                ).astype(BF16)
                back = lax.dot_general(
                    grad, weight_ref[k * channels : (k + 1) * channels, :],
                    (((1,), (1,)), ((), ())), preferred_element_type=F32,
                )
                beyond = jnp.broadcast_to(place[:, k : k + 1], (block, channels)) >= block
                rhs_ref[n * block : (n + 1) * block, :channels] = jnp.where(beyond, 0.0, back).astype(BF16)
                rhs_ref[n * block : (n + 1) * block, channels:] = jnp.where(beyond, back, 0.0).astype(BF16)
            term = jnp.dot(hot_ref[...], rhs_ref[...], preferred_element_type=F32)
            if g == 0:
                acc_ref[...] = term
            else:
                acc_ref[...] += term
        own_ref[pl.ds(q * block, block), :] = acc_ref[:, :channels]
        pieces = (
            (lo_ref, 0), (lo_ref, 1), (lo_ref, 2), (m0_ref, 0),
            (m2_ref, 0), (hi_ref, 0), (hi_ref, 1), (hi_ref, 2),
        )
        for slot, (ref, at) in enumerate(pieces):
            ref[pl.ds(at * high + q * part, part), :] = acc_ref[slot * part : (slot + 1) * part, channels:].astype(BF16)


def backward(row, place, grad, weight, high, block=512, group=3):
    rows, channels = grad.shape
    return pl.pallas_call(
        functools.partial(backward_kernel, group),
        out_shape=(
            jax.ShapeDtypeStruct((rows, channels), F32),
            jax.ShapeDtypeStruct((3 * high, channels), BF16),
            jax.ShapeDtypeStruct((high, channels), BF16),
            jax.ShapeDtypeStruct((high, channels), BF16),
            jax.ShapeDtypeStruct((3 * high, channels), BF16),
        ),
        scratch_shapes=[
            pltpu.VMEM((block, 2 * channels), F32),
            pltpu.VMEM((block, group * block), BF16),
            pltpu.VMEM((group * block, 2 * channels), BF16),
        ],
        compiler_params=pltpu.CompilerParams(vmem_limit_bytes=16 << 20),
        cost_estimate=pl.CostEstimate(flops=TAPS*4*rows*channels*(block+64), bytes_accessed=2<<20, transcendentals=0),
    )(row, place, grad, weight)


def weight_kernel(across, down, group, cols_ref, grad_ref, order_ref, out_ref, line_ref, buffer_ref, sems):
    channels = grad_ref.shape[1]
    eighths = out_ref.shape[1]
    slots = buffer_ref.shape[0]
    steps = TAPS // group

    def fetch(step):
        return pltpu.make_async_copy(
            cols_ref.at[:, pl.ds(step * group * channels, group * channels)],
            buffer_ref.at[step % slots],
            sems.at[step % slots],
        )

    def line(k):
        return (
            slice(k // 8 * channels, (k // 8 + 1) * channels),
            slice(k % 8 * channels, (k % 8 + 1) * channels),
        )

    for step in range(slots - 1):
        fetch(step).start()
    for k in range(TAPS, 8 * eighths):
        line_ref[line(k)] = jnp.zeros((channels, channels), BF16)
    turned = grad_ref[...].T
    for step in range(steps):
        if step + slots - 1 < steps:
            fetch(step + slots - 1).start()
        fetch(step).wait()
        whole = jnp.dot(turned, buffer_ref[step % slots], preferred_element_type=F32)
        for n in range(group):
            line_ref[line(step * group + n)] = (
                whole[:, n * channels : (n + 1) * channels].T.astype(BF16)
            )
    placed = jnp.dot(line_ref[...], order_ref[...], preferred_element_type=F32).astype(BF16)
    for e in range(eighths):
        for x in range(across):
            for y in range(down):
                row = e * channels + x * down
                out_ref[x * down + y, e] = placed[
                    row : row + down, y * channels : (y + 1) * channels
                ]


def weight_terms(cols, grad, order, across, down, group=3, slots=3):
    rows, wide = cols.shape
    channels = wide // TAPS
    eighths = -(-TAPS // 8)
    vmem = pl.BlockSpec(memory_space=pltpu.VMEM)
    return pl.pallas_call(
        functools.partial(weight_kernel, across, down, group),
        in_specs=[pl.BlockSpec(memory_space=pltpu.HBM), vmem, vmem],
        out_specs=vmem,
        out_shape=jax.ShapeDtypeStruct((across * down, eighths, down, channels), BF16),
        scratch_shapes=[
            pltpu.VMEM((eighths * channels, 8 * channels), BF16),
            pltpu.VMEM((slots, rows, group * channels), BF16),
            pltpu.SemaphoreType.DMA((slots,)),
        ],
        compiler_params=pltpu.CompilerParams(vmem_limit_bytes=24 << 20),
        cost_estimate=pl.CostEstimate(
            flops=2 * rows * wide * channels, bytes_accessed=10 << 20, transcendentals=0
        ),
    )(pltpu.with_memory_space_constraint(cols, pltpu.HBM), grad, order)


def from_neighbours(low, mid_low, mid_high, high, arrived=None):
    size = mid_low.shape[0]
    ends_x, ends_y = lax.axis_size("bx") - 1, lax.axis_size("by") - 1
    up_x, down_x = [(i, i + 1) for i in range(ends_x)], [(i + 1, i) for i in range(ends_x)]
    up_y, down_y = [(i, i + 1) for i in range(ends_y)], [(i + 1, i) for i in range(ends_y)]
    a0 = lax.ppermute(high, "bx", up_x)
    a2 = lax.ppermute(low, "bx", down_x)
    if arrived is not None:
        a0, a2, arrived = lax.optimization_barrier((a0, a2, arrived))
    b0 = lax.ppermute(jnp.concatenate([a0[2 * size :], mid_high, a2[2 * size :]]), "by", up_y)
    b2 = lax.ppermute(jnp.concatenate([a0[:size], mid_low, a2[:size]]), "by", down_y)
    return a0, a2, b0, b2, arrived


def everyones(rows):
    devices = lax.axis_size("bx") * lax.axis_size("by")
    copies = jnp.broadcast_to(rows[None], (devices,) + rows.shape)
    return lax.all_to_all(copies, axes, 0, 0, tiled=True)


def per_device(features, live_count, neighbour_map, send_rows, weight, gain, shift, cotangent):
    own_rows = features[0, 0]
    rows_total, channels = own_rows.shape
    size = send_rows.shape[3]
    block_rows = min(rows_total, 512)
    part = size * block_rows // rows_total
    across, down = lax.axis_size("bx"), lax.axis_size("by")
    sent_index = send_rows[0, 0].reshape(-1)
    send_select = (
        sent_index[:, None] == lax.broadcasted_iota(I32, (1, rows_total), 1)
    ).astype(BF16)
    chosen = jnp.dot(send_select, own_rows, preferred_element_type=F32).astype(BF16)
    a0, a2, b0, b2, _ = from_neighbours(
        chosen[: 3 * size], chosen[3 * size : 4 * size], chosen[4 * size : 5 * size], chosen[5 * size :]
    )

    indices = neighbour_map[0, 0]
    block = lax.broadcasted_iota(I32, (1, rows_total), 1) // block_rows
    beyond = indices - rows_total
    target = beyond // size
    inside = beyond - target * size - block * part
    remote = block_rows + (target - (target > 4)) * part + inside
    usable = (inside >= 0) & (inside < part) & (target != 4)
    place = jnp.where(
        indices < rows_total, indices - block * block_rows, jnp.where(usable, remote, -1)
    )
    place = jnp.pad(place, ((0, 5), (0, 0)), constant_values=-1)
    place_down = place.T
    place_rows = place.reshape(-1, rows_total // block_rows, block_rows).transpose(1, 0, 2)

    conv_out, cols = forward(place_down, own_rows, a0, a2, b0, b2, weight)
    conv_float = conv_out.astype(F32)
    live_mask = (lax.broadcasted_iota(I32, (rows_total, 1), 0) < live_count[0, 0]).astype(F32)
    local_count = live_count[0, 0].astype(F32)
    local_mean = jnp.sum(conv_float * live_mask, axis=0) / local_count
    local_dev = (conv_float - local_mean) * live_mask
    local_square = jnp.sum(local_dev * local_dev, axis=0)
    stats = everyones(
        jnp.stack([local_mean, local_square, jnp.full((channels,), local_count)])
    )
    counts = stats[:, 2]
    total_count = jnp.sum(counts, axis=0)
    center = jnp.sum(stats[:, 0] * counts, axis=0) / total_count
    apart = stats[:, 0] - center
    variance = jnp.sum(stats[:, 1] + counts * apart * apart, axis=0) / total_count
    inverse_std = lax.rsqrt(variance + epsilon)
    normalized = (conv_float - center) * inverse_std
    before = gain * normalized + shift
    activated = (jnp.maximum(before, 0.0) * live_mask).astype(BF16)
    upstream = cotangent[0, 0].astype(F32) * (before > 0.0) * live_mask
    sums = everyones(
        jnp.stack([jnp.sum(upstream, axis=0), jnp.sum(upstream * normalized, axis=0)])
    )
    mean_up = jnp.sum(sums[:, 0], axis=0) / total_count
    mean_cross = jnp.sum(sums[:, 1], axis=0) / total_count
    scale = gain * inverse_std
    conv_grad = (
        scale * (upstream - live_mask * (mean_up + normalized * mean_cross))
    ).astype(BF16)

    width = channels // down
    source = lax.broadcasted_iota(I32, (8 * channels, 1), 0)
    spot = lax.broadcasted_iota(I32, (1, down * channels), 1)
    order = (
        source == (spot // width) % 8 * channels + spot // channels * width + spot % width
    ).astype(BF16)
    pieces = weight_terms(cols, conv_grad, order, across, down)
    pieces, conv_grad = lax.optimization_barrier((pieces, conv_grad))
    arrived = lax.all_to_all(pieces, axes, 0, 0, tiled=True)
    own_table, *halo = backward(place_rows, place_down, conv_grad, weight, size)
    a0, a2, b0, b2, arrived = from_neighbours(*halo, arrived)
    slots_back = jnp.concatenate(
        [
            b0[:size], a0[size : 2 * size], b2[:size], b0[size : 2 * size],
            b2[size : 2 * size], b0[2 * size :], a2[size : 2 * size], b2[2 * size :],
        ]
    )
    added_back = lax.dot_general(
        send_select,
        slots_back,
        (((0,), (0,)), ((), ())),
        preferred_element_type=F32,
    )
    own_grad = (own_table + added_back).astype(BF16)
    summed = jnp.sum(arrived.astype(F32), axis=0).reshape(-1, down, 8, width)
    grad_weight = summed.transpose(0, 2, 1, 3).reshape(-1, down, width)[:TAPS] / jnp.sqrt(
        total_count[0]
    )
    return (activated[None, None], own_grad[None, None], grad_weight)


def solution(mesh):
    return jax.shard_map(
        per_device,
        mesh=mesh,
        in_specs=(
            P("bx", "by", None, None),
            P("bx", "by"),
            P("bx", "by", None, None),
            P("bx", "by", None, None),
            P(),
            P(),
            P(),
            P("bx", "by", None, None),
        ),
        out_specs=(P("bx", "by", None, None), P("bx", "by", None, None), P(None, "bx", "by")),
        check_vma=False,
    )
```

```python
import functools

import jax
import jax.numpy as jnp
from jax import lax
from jax.experimental import pallas as pl
from jax.experimental.pallas import tpu as pltpu
from jax.sharding import PartitionSpec as P

epsilon = 1e-05
axes = ("bx", "by")
F32, BF16, I32 = jnp.float32, jnp.bfloat16, jnp.int32
TAPS = 27


def forward_kernel(chunks, place_ref, own_ref, a0_ref, a2_ref, b0_ref, b2_ref, weight_ref, conv_ref, out_ref, win_ref, cols_ref, sems):
    rows, channels = own_ref.shape
    block = win_ref.shape[0]
    part = block // 8
    high = a0_ref.shape[0] // 3
    wide = TAPS // chunks * channels
    lanes = lax.broadcasted_iota(I32, (block, block), 1)

    def copy_out(q, c):
        return pltpu.make_async_copy(
            cols_ref.at[q, :, pl.ds(c * wide, wide)],
            out_ref.at[pl.ds(q * block, block), pl.ds(c * wide, wide)],
            sems.at[q, c],
        )

    def block_step(q, _):
        here = pl.ds(pl.multiple_of(q * block, block), block)
        win_ref[:, :channels] = own_ref[here, :]
        pieces = (
            (b0_ref, 0), (a0_ref, 1), (b2_ref, 0), (b0_ref, 1),
            (b2_ref, 1), (b0_ref, 2), (a2_ref, 1), (b2_ref, 2),
        )
        for slot, (ref, at) in enumerate(pieces):
            win_ref[pl.ds(slot * part, part), channels:] = ref[
                pl.ds(pl.multiple_of(at * high + q * part, part), part), :
            ]
        place = place_ref[here, :]
        for k in range(TAPS):
            column = jnp.broadcast_to(place[:, k : k + 1], (block, channels))
            beyond = column >= block
            inside = jnp.where(beyond, column - block, column)
            hot = jnp.concatenate(
                [
                    jnp.where(inside == lanes[:, c : c + channels], 1.0, 0.0).astype(BF16)
                    for c in range(0, block, channels)
                ],
                axis=1,
            )
            both = jnp.dot(hot, win_ref[...], preferred_element_type=F32)
            cols_ref[q, :, k * channels : (k + 1) * channels] = jnp.where(
                beyond, both[:, channels:], both[:, :channels]
            ).astype(BF16)
            if (k + 1) % (TAPS // chunks) == 0:
                copy_out(q, k // (TAPS // chunks)).start()
        conv_ref[here, :] = jnp.dot(
            cols_ref[q], weight_ref[...], preferred_element_type=F32
        ).astype(BF16)
        return 0

    lax.fori_loop(0, rows // block, block_step, 0)
    for q in range(rows // block):
        for c in range(chunks):
            copy_out(q, c).wait()


def forward(place, own, a0, a2, b0, b2, weight, block=512, chunks=3):
    rows, channels = own.shape
    vmem = pl.BlockSpec(memory_space=pltpu.VMEM)
    return pl.pallas_call(
        functools.partial(forward_kernel, chunks),
        in_specs=[vmem] * 7,
        out_specs=(vmem, pl.BlockSpec(memory_space=pltpu.HBM)),
        out_shape=(
            jax.ShapeDtypeStruct((rows, channels), BF16),
            pltpu.HBM((rows, TAPS * channels), BF16),
        ),
        scratch_shapes=[
            pltpu.VMEM((block, 2 * channels), BF16),
            pltpu.VMEM((rows // block, block, TAPS * channels), BF16),
            pltpu.SemaphoreType.DMA((rows // block, chunks)),
        ],
        compiler_params=pltpu.CompilerParams(vmem_limit_bytes=20 << 20),
        cost_estimate=pl.CostEstimate(
            flops=TAPS * 4 * rows * channels * block, bytes_accessed=9 << 20, transcendentals=0
        ),
    )(place, own, a0, a2, b0, b2, weight)


def backward_kernel(group, row_ref, place_ref, grad_ref, table_ref, own_ref, lo_ref, m0_ref, m2_ref, hi_ref, acc_ref, hot_ref, rhs_ref, weight_ref, sems):
    rows, channels = grad_ref.shape
    block = acc_ref.shape[0]
    part = block // 8
    high = m0_ref.shape[0]
    steps = TAPS // group
    wide = group * channels

    def fetch(step):
        here = pl.ds(step * wide, wide)
        return pltpu.make_async_copy(table_ref.at[here, :], weight_ref.at[here, :], sems.at[step])

    for step in range(steps):
        fetch(step).start()
    for q in range(rows // block):
        grad = grad_ref[pl.ds(q * block, block), :]
        place = place_ref[pl.ds(q * block, block), :]
        down = lax.broadcasted_iota(I32, (block, block), 0)
        for g in range(steps):
            if q == 0:
                fetch(g).wait()
            for n in range(group):
                k = g * group + n
                line = row_ref[q, k : k + 1, :]
                line = jnp.where(line >= block, line - block, line)
                hot_ref[:, n * block : (n + 1) * block] = jnp.where(
                    jnp.broadcast_to(line, (block, block)) == down, 1.0, 0.0
                ).astype(BF16)
                back = lax.dot_general(
                    grad, weight_ref[k * channels : (k + 1) * channels, :],
                    (((1,), (1,)), ((), ())), preferred_element_type=F32,
                )
                beyond = jnp.broadcast_to(place[:, k : k + 1], (block, channels)) >= block
                rhs_ref[n * block : (n + 1) * block, :channels] = jnp.where(beyond, 0.0, back).astype(BF16)
                rhs_ref[n * block : (n + 1) * block, channels:] = jnp.where(beyond, back, 0.0).astype(BF16)
            term = jnp.dot(hot_ref[...], rhs_ref[...], preferred_element_type=F32)
            if g == 0:
                acc_ref[...] = term
            else:
                acc_ref[...] += term
        own_ref[pl.ds(q * block, block), :] = acc_ref[:, :channels]
        pieces = (
            (lo_ref, 0), (lo_ref, 1), (lo_ref, 2), (m0_ref, 0),
            (m2_ref, 0), (hi_ref, 0), (hi_ref, 1), (hi_ref, 2),
        )
        for slot, (ref, at) in enumerate(pieces):
            ref[pl.ds(at * high + q * part, part), :] = acc_ref[slot * part : (slot + 1) * part, channels:].astype(BF16)


def backward(row, place, grad, weight, high, block=512, group=3):
    rows, channels = grad.shape
    vmem = pl.BlockSpec(memory_space=pltpu.VMEM)
    return pl.pallas_call(
        functools.partial(backward_kernel, group),
        in_specs=[vmem, vmem, vmem, pl.BlockSpec(memory_space=pltpu.HBM)],
        out_shape=(
            jax.ShapeDtypeStruct((rows, channels), F32),
            jax.ShapeDtypeStruct((3 * high, channels), BF16),
            jax.ShapeDtypeStruct((high, channels), BF16),
            jax.ShapeDtypeStruct((high, channels), BF16),
            jax.ShapeDtypeStruct((3 * high, channels), BF16),
        ),
        scratch_shapes=[
            pltpu.VMEM((block, 2 * channels), F32),
            pltpu.VMEM((block, group * block), BF16),
            pltpu.VMEM((group * block, 2 * channels), BF16),
            pltpu.VMEM(weight.shape, BF16),
            pltpu.SemaphoreType.DMA((TAPS // group,)),
        ],
        compiler_params=pltpu.CompilerParams(vmem_limit_bytes=16 << 20),
        cost_estimate=pl.CostEstimate(flops=TAPS*4*rows*channels*(block+64), bytes_accessed=2<<20, transcendentals=0),
    )(row, place, grad, pltpu.with_memory_space_constraint(weight, pltpu.HBM))


def product_kernel(group, extra, cols_ref, rhs_ref, out_ref, left_ref, whole_ref, buffer_ref, in_sems, out_sems):
    channels = rhs_ref.shape[1]
    wide = group * channels
    slots = buffer_ref.shape[0]
    steps = TAPS // group

    def fetch(step):
        return pltpu.make_async_copy(
            cols_ref.at[:, pl.ds(step * wide, wide)],
            buffer_ref.at[step % slots],
            in_sems.at[step % slots],
        )

    def leave(step):
        here = pl.ds(step * wide, wide)
        return pltpu.make_async_copy(
            whole_ref.at[:, here], out_ref.at[:, here], out_sems.at[step]
        )

    for step in range(slots - 1):
        fetch(step).start()
    left_ref[:channels, :] = rhs_ref[...].T
    if extra:
        left_ref[channels:, :] = jnp.ones((extra, left_ref.shape[1]), BF16)
    for step in range(steps):
        if step + slots - 1 < steps:
            fetch(step + slots - 1).start()
        fetch(step).wait()
        whole_ref[:, step * wide : (step + 1) * wide] = jnp.dot(
            left_ref[...], buffer_ref[step % slots], preferred_element_type=F32
        )
        leave(step).start()
    for step in range(steps):
        leave(step).wait()


def product(cols, rhs, extra=0, group=3, slots=3):
    rows, wide = cols.shape
    channels = rhs.shape[1]
    hbm = pl.BlockSpec(memory_space=pltpu.HBM)
    return pl.pallas_call(
        functools.partial(product_kernel, group, extra),
        in_specs=[hbm, pl.BlockSpec(memory_space=pltpu.VMEM)],
        out_specs=hbm,
        out_shape=pltpu.HBM((channels + extra, wide), F32),
        scratch_shapes=[
            pltpu.VMEM((channels + extra, rows), BF16),
            pltpu.VMEM((channels + extra, wide), F32),
            pltpu.VMEM((slots, rows, group * channels), BF16),
            pltpu.SemaphoreType.DMA((slots,)),
            pltpu.SemaphoreType.DMA((TAPS // group,)),
        ],
        compiler_params=pltpu.CompilerParams(vmem_limit_bytes=16 << 20),
        cost_estimate=pl.CostEstimate(
            flops=2 * rows * wide * channels, bytes_accessed=9 << 20, transcendentals=0
        ),
    )(pltpu.with_memory_space_constraint(cols, pltpu.HBM), rhs)


def weight_kernel(across, down, group, up_ref, conv_ref, scale_ref, order_ref, out_ref, line_ref, first_ref, second_ref, sems):
    channels = scale_ref.shape[1]
    eighths = out_ref.shape[1]
    wide = group * channels
    steps = TAPS // group

    def fetch(step):
        here = pl.ds(step * wide, wide)
        return (
            pltpu.make_async_copy(up_ref.at[:, here], first_ref.at[:, here], sems.at[0, step]),
            pltpu.make_async_copy(conv_ref.at[:, here], second_ref.at[:, here], sems.at[1, step]),
        )

    def line(k):
        return (
            slice(k // 8 * channels, (k // 8 + 1) * channels),
            slice(k % 8 * channels, (k % 8 + 1) * channels),
        )

    for step in range(steps):
        for copy in fetch(step):
            copy.start()
    for k in range(TAPS, 8 * eighths):
        line_ref[line(k)] = jnp.zeros((channels, channels), BF16)
    turned = scale_ref[...].T
    scales = [jnp.broadcast_to(turned[:, n : n + 1], (channels, channels)) for n in range(3)]
    for step in range(steps):
        for copy in fetch(step):
            copy.wait()
        for k in range(step * group, (step + 1) * group):
            here = slice(k * channels, (k + 1) * channels)
            term = (
                scales[0] * first_ref[:, here]
                - scales[1] * second_ref[channels : channels + 1, here]
                - scales[2] * second_ref[:channels, here]
            )
            line_ref[line(k)] = term.T.astype(BF16)
    placed = jnp.dot(line_ref[...], order_ref[...], preferred_element_type=F32).astype(BF16)
    for e in range(eighths):
        for x in range(across):
            for y in range(down):
                row = e * channels + x * down
                out_ref[x * down + y, e] = placed[
                    row : row + down, y * channels : (y + 1) * channels
                ]


def weight_terms(up_part, conv_part, scales, order, across, down, group=3):
    channels, wide = up_part.shape
    eighths = -(-TAPS // 8)
    vmem, hbm = pl.BlockSpec(memory_space=pltpu.VMEM), pl.BlockSpec(memory_space=pltpu.HBM)
    return pl.pallas_call(
        functools.partial(weight_kernel, across, down, group),
        in_specs=[hbm, hbm, vmem, vmem],
        out_specs=vmem,
        out_shape=jax.ShapeDtypeStruct((across * down, eighths, down, channels), BF16),
        scratch_shapes=[
            pltpu.VMEM((eighths * channels, 8 * channels), BF16),
            pltpu.VMEM(up_part.shape, F32),
            pltpu.VMEM(conv_part.shape, F32),
            pltpu.SemaphoreType.DMA((2, TAPS // group)),
        ],
        compiler_params=pltpu.CompilerParams(vmem_limit_bytes=16 << 20),
        cost_estimate=pl.CostEstimate(flops=1 << 30, bytes_accessed=5 << 20, transcendentals=0),
    )(
        pltpu.with_memory_space_constraint(up_part, pltpu.HBM),
        pltpu.with_memory_space_constraint(conv_part, pltpu.HBM),
        scales,
        order,
    )


def add_back_kernel(index_ref, a0_ref, a2_ref, b0_ref, b2_ref, own_ref, out_ref, hot_ref, slot_ref):
    rows, channels = own_ref.shape
    slots, size = index_ref.shape
    down = lax.broadcasted_iota(I32, (rows, size), 0)
    pieces = (
        (b0_ref, 0), (a0_ref, 1), (b2_ref, 0), (b0_ref, 1),
        (b2_ref, 1), (b0_ref, 2), (a2_ref, 1), (b2_ref, 2),
    )
    for slot, (ref, at) in enumerate(pieces):
        slot_ref[slot * size : (slot + 1) * size, :] = ref[at * size : (at + 1) * size, :]
        hot_ref[:, slot * size : (slot + 1) * size] = jnp.where(
            jnp.broadcast_to(index_ref[slot : slot + 1, :], (rows, size)) == down, 1.0, 0.0
        ).astype(BF16)
    added = jnp.dot(hot_ref[...], slot_ref[...], preferred_element_type=F32)
    out_ref[...] = (own_ref[...] + added).astype(BF16)


def add_back(index, a0, a2, b0, b2, own):
    rows, channels = own.shape
    return pl.pallas_call(
        add_back_kernel,
        out_shape=jax.ShapeDtypeStruct((rows, channels), BF16),
        scratch_shapes=[
            pltpu.VMEM((rows, index.size), BF16),
            pltpu.VMEM((index.size, channels), BF16),
        ],
        compiler_params=pltpu.CompilerParams(vmem_limit_bytes=16 << 20),
        cost_estimate=pl.CostEstimate(
            flops=2 * rows * rows * channels, bytes_accessed=2 << 20, transcendentals=0
        ),
    )(index, a0, a2, b0, b2, own)


def from_neighbours(low, mid_low, mid_high, high, arrived):
    size = mid_low.shape[0]
    ends_x, ends_y = lax.axis_size("bx") - 1, lax.axis_size("by") - 1
    up_x, down_x = [(i, i + 1) for i in range(ends_x)], [(i + 1, i) for i in range(ends_x)]
    up_y, down_y = [(i, i + 1) for i in range(ends_y)], [(i + 1, i) for i in range(ends_y)]
    a0 = lax.ppermute(high, "bx", up_x)
    a2 = lax.ppermute(low, "bx", down_x)
    a0, a2, arrived = lax.optimization_barrier((a0, a2, arrived))
    b0 = lax.ppermute(jnp.concatenate([a0[2 * size :], mid_high, a2[2 * size :]]), "by", up_y)
    b2 = lax.ppermute(jnp.concatenate([a0[:size], mid_low, a2[:size]]), "by", down_y)
    return a0, a2, b0, b2, arrived


def everyones(rows):
    devices = lax.axis_size("bx") * lax.axis_size("by")
    copies = jnp.broadcast_to(rows[None], (devices,) + rows.shape)
    return lax.all_to_all(copies, axes, 0, 0, tiled=True)


def per_device(features, live_count, neighbour_map, send_rows, weight, gain, shift, cotangent):
    own_rows = features[0, 0]
    rows_total, channels = own_rows.shape
    size = send_rows.shape[3]
    block_rows = min(rows_total, 512)
    part = size * block_rows // rows_total
    across, down = lax.axis_size("bx"), lax.axis_size("by")
    sent_index = send_rows[0, 0].reshape(-1)
    send_select = (
        sent_index[:, None] == lax.broadcasted_iota(I32, (1, rows_total), 1)
    ).astype(BF16)
    chosen = jnp.dot(send_select, own_rows, preferred_element_type=F32).astype(BF16)
    a0, a2, b0, b2, indices = from_neighbours(
        chosen[: 3 * size],
        chosen[3 * size : 4 * size],
        chosen[4 * size : 5 * size],
        chosen[5 * size :],
        neighbour_map[0, 0],
    )

    block = lax.broadcasted_iota(I32, (1, rows_total), 1) // block_rows
    beyond = indices - rows_total
    target = beyond // size
    inside = beyond - target * size - block * part
    remote = block_rows + (target - (target > 4)) * part + inside
    usable = (inside >= 0) & (inside < part) & (target != 4)
    place = jnp.where(
        indices < rows_total, indices - block * block_rows, jnp.where(usable, remote, -1)
    )
    place = jnp.pad(place, ((0, 5), (0, 0)), constant_values=-1)
    place_down = place.T
    place_rows = place.reshape(-1, rows_total // block_rows, block_rows).transpose(1, 0, 2)

    conv_out, cols = forward(place_down, own_rows, a0, a2, b0, b2, weight)
    conv_float = conv_out.astype(F32)
    live_mask = (lax.broadcasted_iota(I32, (rows_total, 1), 0) < live_count[0, 0]).astype(F32)
    local_count = live_count[0, 0].astype(F32)
    local_mean = jnp.sum(conv_float * live_mask, axis=0) / local_count
    local_dev = (conv_float - local_mean) * live_mask
    local_square = jnp.sum(local_dev * local_dev, axis=0)
    stats = everyones(
        jnp.stack([local_mean, local_square, jnp.full((channels,), local_count)])
    )
    conv_part = product(cols, conv_out, extra=16)
    stats, place_rows, conv_part = lax.optimization_barrier((stats, place_rows, conv_part))
    counts = stats[:, 2]
    total_count = jnp.sum(counts, axis=0)
    center = jnp.sum(stats[:, 0] * counts, axis=0) / total_count
    apart = stats[:, 0] - center
    variance = jnp.sum(stats[:, 1] + counts * apart * apart, axis=0) / total_count
    inverse_std = lax.rsqrt(variance + epsilon)
    normalized = (conv_float - center) * inverse_std
    before = gain * normalized + shift
    activated = (jnp.maximum(before, 0.0) * live_mask).astype(BF16)
    upstream = cotangent[0, 0].astype(F32) * (before > 0.0) * live_mask
    sums = everyones(
        jnp.stack([jnp.sum(upstream, axis=0), jnp.sum(upstream * normalized, axis=0)])
    )
    up_part = product(cols, upstream.astype(BF16))
    sums, up_part = lax.optimization_barrier((sums, up_part))
    mean_up = jnp.sum(sums[:, 0], axis=0) / total_count
    mean_cross = jnp.sum(sums[:, 1], axis=0) / total_count
    scale = gain * inverse_std
    conv_grad = (
        scale * (upstream - live_mask * (mean_up + normalized * mean_cross))
    ).astype(BF16)

    width = channels // down
    source = lax.broadcasted_iota(I32, (8 * channels, 1), 0)
    spot = lax.broadcasted_iota(I32, (1, down * channels), 1)
    order = (
        source == (spot // width) % 8 * channels + spot // channels * width + spot % width
    ).astype(BF16)
    scales = jnp.stack(
        [
            scale,
            scale * (mean_up - mean_cross * inverse_std * center),
            scale * mean_cross * inverse_std,
        ]
        + [jnp.zeros_like(scale)] * 5
    )
    pieces = weight_terms(up_part, conv_part, scales, order, across, down)
    pieces, conv_grad = lax.optimization_barrier((pieces, conv_grad))
    arrived = lax.all_to_all(pieces, axes, 0, 0, tiled=True)
    own_table, *halo = backward(place_rows, place_down, conv_grad, weight, size)
    a0, a2, b0, b2, arrived = from_neighbours(*halo, arrived)
    own_grad = add_back(send_rows[0, 0], a0, a2, b0, b2, own_table)
    summed = jnp.sum(arrived.astype(F32), axis=0).reshape(-1, down, 8, width)
    grad_weight = summed.transpose(0, 2, 1, 3).reshape(-1, down, width)[:TAPS] / jnp.sqrt(
        total_count[0]
    )
    return (activated[None, None], own_grad[None, None], grad_weight)


def solution(mesh):
    return jax.shard_map(
        per_device,
        mesh=mesh,
        in_specs=(
            P("bx", "by", None, None),
            P("bx", "by"),
            P("bx", "by", None, None),
            P("bx", "by", None, None),
            P(),
            P(),
            P(),
            P("bx", "by", None, None),
        ),
        out_specs=(P("bx", "by", None, None), P("bx", "by", None, None), P(None, "bx", "by")),
        check_vma=False,
    )
```

```python
import functools

import jax
import jax.numpy as jnp
from jax import lax
from jax.experimental import pallas as pl
from jax.experimental.pallas import tpu as pltpu
from jax.sharding import PartitionSpec as P

epsilon = 1e-05
axes = ("bx", "by")
F32, BF16, I32 = jnp.float32, jnp.bfloat16, jnp.int32
TAPS = 27


def forward_kernel(chunks, place_ref, own_ref, a0_ref, a2_ref, b0_ref, b2_ref, weight_ref, conv_ref, out_ref, win_ref, cols_ref, sems):
    rows, channels = own_ref.shape
    block = win_ref.shape[0]
    part = block // 8
    high = a0_ref.shape[0] // 3
    wide = TAPS // chunks * channels
    lanes = lax.broadcasted_iota(I32, (block, block), 1)

    def copy_out(q, c):
        return pltpu.make_async_copy(
            cols_ref.at[q, :, pl.ds(c * wide, wide)],
            out_ref.at[pl.ds(q * block, block), pl.ds(c * wide, wide)],
            sems.at[q, c],
        )

    def block_step(q, _):
        here = pl.ds(pl.multiple_of(q * block, block), block)
        win_ref[:, :channels] = own_ref[here, :]
        pieces = (
            (b0_ref, 0), (a0_ref, 1), (b2_ref, 0), (b0_ref, 1),
            (b2_ref, 1), (b0_ref, 2), (a2_ref, 1), (b2_ref, 2),
        )
        for slot, (ref, at) in enumerate(pieces):
            win_ref[pl.ds(slot * part, part), channels:] = ref[
                pl.ds(pl.multiple_of(at * high + q * part, part), part), :
            ]
        place = place_ref[here, :]
        for k in range(TAPS):
            column = jnp.broadcast_to(place[:, k : k + 1], (block, channels))
            beyond = column >= block
            inside = jnp.where(beyond, column - block, column)
            hot = jnp.concatenate(
                [
                    jnp.where(inside == lanes[:, c : c + channels], 1.0, 0.0).astype(BF16)
                    for c in range(0, block, channels)
                ],
                axis=1,
            )
            both = jnp.dot(hot, win_ref[...], preferred_element_type=F32)
            cols_ref[q, :, k * channels : (k + 1) * channels] = jnp.where(
                beyond, both[:, channels:], both[:, :channels]
            ).astype(BF16)
            if (k + 1) % (TAPS // chunks) == 0:
                copy_out(q, k // (TAPS // chunks)).start()
        conv_ref[here, :] = jnp.dot(
            cols_ref[q], weight_ref[...], preferred_element_type=F32
        ).astype(BF16)
        return 0

    lax.fori_loop(0, rows // block, block_step, 0)
    for q in range(rows // block):
        for c in range(chunks):
            copy_out(q, c).wait()


def forward(place, own, a0, a2, b0, b2, weight, block=512, chunks=3):
    rows, channels = own.shape
    vmem = pl.BlockSpec(memory_space=pltpu.VMEM)
    return pl.pallas_call(
        functools.partial(forward_kernel, chunks),
        in_specs=[vmem] * 7,
        out_specs=(vmem, pl.BlockSpec(memory_space=pltpu.HBM)),
        out_shape=(
            jax.ShapeDtypeStruct((rows, channels), BF16),
            pltpu.HBM((rows, TAPS * channels), BF16),
        ),
        scratch_shapes=[
            pltpu.VMEM((block, 2 * channels), BF16),
            pltpu.VMEM((rows // block, block, TAPS * channels), BF16),
            pltpu.SemaphoreType.DMA((rows // block, chunks)),
        ],
        compiler_params=pltpu.CompilerParams(vmem_limit_bytes=20 << 20),
        cost_estimate=pl.CostEstimate(
            flops=TAPS * 4 * rows * channels * block, bytes_accessed=9 << 20, transcendentals=0
        ),
    )(place, own, a0, a2, b0, b2, weight)


def backward_kernel(group, row_ref, place_ref, grad_ref, weight_ref, own_ref, lo_ref, m0_ref, m2_ref, hi_ref, acc_ref, hot_ref, rhs_ref):
    rows, channels = grad_ref.shape
    block = acc_ref.shape[0]
    part = block // 8
    high = m0_ref.shape[0]
    for q in range(rows // block):
        grad = grad_ref[pl.ds(q * block, block), :]
        place = place_ref[pl.ds(q * block, block), :]
        down = lax.broadcasted_iota(I32, (block, block), 0)
        for g in range(TAPS // group):
            for n in range(group):
                k = g * group + n
                line = row_ref[q, k : k + 1, :]
                line = jnp.where(line >= block, line - block, line)
                hot_ref[:, n * block : (n + 1) * block] = jnp.where(
                    jnp.broadcast_to(line, (block, block)) == down, 1.0, 0.0
                ).astype(BF16)
                back = lax.dot_general(
                    grad, weight_ref[k * channels : (k + 1) * channels, :],
                    (((1,), (1,)), ((), ())), preferred_element_type=F32,
                )
                beyond = jnp.broadcast_to(place[:, k : k + 1], (block, channels)) >= block
                rhs_ref[n * block : (n + 1) * block, :channels] = jnp.where(beyond, 0.0, back).astype(BF16)
                rhs_ref[n * block : (n + 1) * block, channels:] = jnp.where(beyond, back, 0.0).astype(BF16)
            term = jnp.dot(hot_ref[...], rhs_ref[...], preferred_element_type=F32)
            if g == 0:
                acc_ref[...] = term
            else:
                acc_ref[...] += term
        own_ref[pl.ds(q * block, block), :] = acc_ref[:, :channels]
        pieces = (
            (lo_ref, 0), (lo_ref, 1), (lo_ref, 2), (m0_ref, 0),
            (m2_ref, 0), (hi_ref, 0), (hi_ref, 1), (hi_ref, 2),
        )
        for slot, (ref, at) in enumerate(pieces):
            ref[pl.ds(at * high + q * part, part), :] = acc_ref[slot * part : (slot + 1) * part, channels:].astype(BF16)


def backward(row, place, grad, weight, high, block=512, group=3):
    rows, channels = grad.shape
    return pl.pallas_call(
        functools.partial(backward_kernel, group),
        out_shape=(
            jax.ShapeDtypeStruct((rows, channels), F32),
            jax.ShapeDtypeStruct((3 * high, channels), BF16),
            jax.ShapeDtypeStruct((high, channels), BF16),
            jax.ShapeDtypeStruct((high, channels), BF16),
            jax.ShapeDtypeStruct((3 * high, channels), BF16),
        ),
        scratch_shapes=[
            pltpu.VMEM((block, 2 * channels), F32),
            pltpu.VMEM((block, group * block), BF16),
            pltpu.VMEM((group * block, 2 * channels), BF16),
        ],
        compiler_params=pltpu.CompilerParams(vmem_limit_bytes=16 << 20),
        cost_estimate=pl.CostEstimate(flops=TAPS*4*rows*channels*(block+64), bytes_accessed=2<<20, transcendentals=0),
    )(row, place, grad, weight)


def product_kernel(group, extra, cols_ref, rhs_ref, out_ref, left_ref, whole_ref, buffer_ref, in_sems, out_sems):
    channels = rhs_ref.shape[1]
    wide = group * channels
    slots = buffer_ref.shape[0]
    steps = TAPS // group

    def fetch(step):
        return pltpu.make_async_copy(
            cols_ref.at[:, pl.ds(step * wide, wide)],
            buffer_ref.at[step % slots],
            in_sems.at[step % slots],
        )

    def leave(step):
        here = pl.ds(step * wide, wide)
        return pltpu.make_async_copy(
            whole_ref.at[:, here], out_ref.at[:, here], out_sems.at[step]
        )

    for step in range(slots - 1):
        fetch(step).start()
    left_ref[:channels, :] = rhs_ref[...].T
    if extra:
        left_ref[channels:, :] = jnp.ones((extra, left_ref.shape[1]), BF16)
    for step in range(steps):
        if step + slots - 1 < steps:
            fetch(step + slots - 1).start()
        fetch(step).wait()
        whole_ref[:, step * wide : (step + 1) * wide] = jnp.dot(
            left_ref[...], buffer_ref[step % slots], preferred_element_type=F32
        )
        leave(step).start()
    for step in range(steps):
        leave(step).wait()


def product(cols, rhs, extra=0, group=3, slots=3):
    rows, wide = cols.shape
    channels = rhs.shape[1]
    hbm = pl.BlockSpec(memory_space=pltpu.HBM)
    return pl.pallas_call(
        functools.partial(product_kernel, group, extra),
        in_specs=[hbm, pl.BlockSpec(memory_space=pltpu.VMEM)],
        out_specs=hbm,
        out_shape=pltpu.HBM((channels + extra, wide), F32),
        scratch_shapes=[
            pltpu.VMEM((channels + extra, rows), BF16),
            pltpu.VMEM((channels + extra, wide), F32),
            pltpu.VMEM((slots, rows, group * channels), BF16),
            pltpu.SemaphoreType.DMA((slots,)),
            pltpu.SemaphoreType.DMA((TAPS // group,)),
        ],
        compiler_params=pltpu.CompilerParams(vmem_limit_bytes=16 << 20),
        cost_estimate=pl.CostEstimate(
            flops=2 * rows * wide * channels, bytes_accessed=9 << 20, transcendentals=0
        ),
    )(pltpu.with_memory_space_constraint(cols, pltpu.HBM), rhs)


def weight_kernel(across, down, group, live_ref, sums_ref, batch_ref, upstream_ref, conv_out_ref, up_ref, conv_ref, order_ref, pieces_ref, grad_out_ref, line_ref, first_ref, second_ref, out_ref, grad_ref, sems, out_sems):
    rows, channels = grad_ref.shape
    eighths = pieces_ref.shape[1]
    wide = group * channels
    steps = TAPS // group

    def fetch(step):
        here = pl.ds(step * wide, wide)
        return (
            pltpu.make_async_copy(up_ref.at[:, here], first_ref.at[:, here], sems.at[0, step]),
            pltpu.make_async_copy(conv_ref.at[:, here], second_ref.at[:, here], sems.at[1, step]),
        )

    def line(k):
        return (
            slice(k // 8 * channels, (k // 8 + 1) * channels),
            slice(k % 8 * channels, (k % 8 + 1) * channels),
        )

    for step in range(steps):
        for copy in fetch(step):
            copy.start()
    for k in range(TAPS, 8 * eighths):
        line_ref[line(k)] = jnp.zeros((channels, channels), BF16)
    grad_copy = pltpu.make_async_copy(grad_ref, grad_out_ref, out_sems.at[eighths])
    scale, inverse_std, center, total = [batch_ref[n : n + 1, :] for n in range(4)]
    sums = jnp.sum(sums_ref[...], axis=0)
    mean_up, mean_cross = sums[0:1] / total, sums[1:2] / total
    live = lax.broadcasted_iota(I32, (rows, channels), 0) < live_ref[0, 0]
    normalized = (conv_out_ref[...].astype(F32) - center) * inverse_std
    grad_ref[...] = (
        scale
        * (
            upstream_ref[...].astype(F32)
            - jnp.where(live, mean_up + normalized * mean_cross, 0.0)
        )
    ).astype(BF16)
    grad_copy.start()
    per_cross = scale * mean_cross * inverse_std
    turned = jnp.concatenate(
        [scale, scale * mean_up - per_cross * center, per_cross]
        + [jnp.zeros((5, channels), F32)],
        axis=0,
    ).T
    scales = [jnp.broadcast_to(turned[:, n : n + 1], (channels, channels)) for n in range(3)]
    for step in range(steps):
        for copy in fetch(step):
            copy.wait()
        for k in range(step * group, (step + 1) * group):
            here = slice(k * channels, (k + 1) * channels)
            term = (
                scales[0] * first_ref[:, here]
                - scales[1] * second_ref[channels : channels + 1, here]
                - scales[2] * second_ref[:channels, here]
            )
            line_ref[line(k)] = term.T.astype(BF16)
    placed = jnp.dot(line_ref[...], order_ref[...], preferred_element_type=F32).astype(BF16)
    copies = []
    for e in range(eighths):
        for x in range(across):
            for y in range(down):
                row = e * channels + x * down
                out_ref[x * down + y, e] = placed[
                    row : row + down, y * channels : (y + 1) * channels
                ]
        copies.append(
            pltpu.make_async_copy(out_ref.at[:, e], pieces_ref.at[:, e], out_sems.at[e])
        )
        copies[e].start()
    for copy in copies:
        copy.wait()
    grad_copy.wait()


def weight_terms(live, sums, batch, upstream, conv_out, up_part, conv_part, order, across, down, group=3):
    channels, wide = up_part.shape
    eighths = -(-TAPS // 8)
    vmem, hbm = pl.BlockSpec(memory_space=pltpu.VMEM), pl.BlockSpec(memory_space=pltpu.HBM)
    return pl.pallas_call(
        functools.partial(weight_kernel, across, down, group),
        in_specs=[pl.BlockSpec(memory_space=pltpu.SMEM), vmem, vmem, vmem, vmem, hbm, hbm, vmem],
        out_specs=(hbm, hbm),
        out_shape=(
            pltpu.HBM((across * down, eighths, down, channels), BF16),
            pltpu.HBM(upstream.shape, BF16),
        ),
        scratch_shapes=[
            pltpu.VMEM((eighths * channels, 8 * channels), BF16),
            pltpu.VMEM(up_part.shape, F32),
            pltpu.VMEM(conv_part.shape, F32),
            pltpu.VMEM((across * down, eighths, down, channels), BF16),
            pltpu.VMEM(upstream.shape, BF16),
            pltpu.SemaphoreType.DMA((2, TAPS // group)),
            pltpu.SemaphoreType.DMA((eighths + 1,)),
        ],
        compiler_params=pltpu.CompilerParams(vmem_limit_bytes=20 << 20),
        cost_estimate=pl.CostEstimate(flops=1 << 30, bytes_accessed=5 << 20, transcendentals=0),
    )(
        live,
        sums,
        batch,
        upstream,
        conv_out,
        pltpu.with_memory_space_constraint(up_part, pltpu.HBM),
        pltpu.with_memory_space_constraint(conv_part, pltpu.HBM),
        order,
    )


def add_back_kernel(index_ref, a0_ref, a2_ref, b0_ref, b2_ref, own_ref, out_ref, hot_ref, slot_ref):
    rows, channels = own_ref.shape
    slots, size = index_ref.shape
    down = lax.broadcasted_iota(I32, (rows, size), 0)
    pieces = (
        (b0_ref, 0), (a0_ref, 1), (b2_ref, 0), (b0_ref, 1),
        (b2_ref, 1), (b0_ref, 2), (a2_ref, 1), (b2_ref, 2),
    )
    for slot, (ref, at) in enumerate(pieces):
        slot_ref[slot * size : (slot + 1) * size, :] = ref[at * size : (at + 1) * size, :]
        hot_ref[:, slot * size : (slot + 1) * size] = jnp.where(
            jnp.broadcast_to(index_ref[slot : slot + 1, :], (rows, size)) == down, 1.0, 0.0
        ).astype(BF16)
    added = jnp.dot(hot_ref[...], slot_ref[...], preferred_element_type=F32)
    out_ref[...] = (own_ref[...] + added).astype(BF16)


def add_back(index, a0, a2, b0, b2, own):
    rows, channels = own.shape
    return pl.pallas_call(
        add_back_kernel,
        out_shape=jax.ShapeDtypeStruct((rows, channels), BF16),
        scratch_shapes=[
            pltpu.VMEM((rows, index.size), BF16),
            pltpu.VMEM((index.size, channels), BF16),
        ],
        compiler_params=pltpu.CompilerParams(vmem_limit_bytes=16 << 20),
        cost_estimate=pl.CostEstimate(
            flops=2 * rows * rows * channels, bytes_accessed=2 << 20, transcendentals=0
        ),
    )(index, a0, a2, b0, b2, own)


def from_neighbours(low, mid_low, mid_high, high, arrived):
    size = mid_low.shape[0]
    ends_x, ends_y = lax.axis_size("bx") - 1, lax.axis_size("by") - 1
    up_x, down_x = [(i, i + 1) for i in range(ends_x)], [(i + 1, i) for i in range(ends_x)]
    up_y, down_y = [(i, i + 1) for i in range(ends_y)], [(i + 1, i) for i in range(ends_y)]
    a0 = lax.ppermute(high, "bx", up_x)
    a2 = lax.ppermute(low, "bx", down_x)
    a0, a2, arrived = lax.optimization_barrier((a0, a2, arrived))
    b0 = lax.ppermute(jnp.concatenate([a0[2 * size :], mid_high, a2[2 * size :]]), "by", up_y)
    b2 = lax.ppermute(jnp.concatenate([a0[:size], mid_low, a2[:size]]), "by", down_y)
    return a0, a2, b0, b2, arrived


def everyones(rows):
    devices = lax.axis_size("bx") * lax.axis_size("by")
    copies = jnp.broadcast_to(rows[None], (devices,) + rows.shape)
    return lax.all_to_all(copies, axes, 0, 0, tiled=True)


def per_device(features, live_count, neighbour_map, send_rows, weight, gain, shift, cotangent):
    own_rows = features[0, 0]
    rows_total, channels = own_rows.shape
    size = send_rows.shape[3]
    block_rows = min(rows_total, 512)
    part = size * block_rows // rows_total
    across, down = lax.axis_size("bx"), lax.axis_size("by")
    sent_index = send_rows[0, 0].reshape(-1)
    send_select = (
        sent_index[:, None] == lax.broadcasted_iota(I32, (1, rows_total), 1)
    ).astype(BF16)
    chosen = jnp.dot(send_select, own_rows, preferred_element_type=F32).astype(BF16)
    a0, a2, b0, b2, indices = from_neighbours(
        chosen[: 3 * size],
        chosen[3 * size : 4 * size],
        chosen[4 * size : 5 * size],
        chosen[5 * size :],
        neighbour_map[0, 0],
    )

    block = lax.broadcasted_iota(I32, (1, rows_total), 1) // block_rows
    beyond = indices - rows_total
    target = beyond // size
    inside = beyond - target * size - block * part
    remote = block_rows + (target - (target > 4)) * part + inside
    usable = (inside >= 0) & (inside < part) & (target != 4)
    place = jnp.where(
        indices < rows_total, indices - block * block_rows, jnp.where(usable, remote, -1)
    )
    place = jnp.pad(place, ((0, 5), (0, 0)), constant_values=-1)
    place_down = place.T
    place_rows = place.reshape(-1, rows_total // block_rows, block_rows).transpose(1, 0, 2)

    conv_out, cols = forward(place_down, own_rows, a0, a2, b0, b2, weight)
    conv_float = conv_out.astype(F32)
    live_mask = (lax.broadcasted_iota(I32, (rows_total, 1), 0) < live_count[0, 0]).astype(F32)
    local_count = live_count[0, 0].astype(F32)
    local_mean = jnp.sum(conv_float * live_mask, axis=0) / local_count
    local_dev = (conv_float - local_mean) * live_mask
    local_square = jnp.sum(local_dev * local_dev, axis=0)
    stats = everyones(
        jnp.stack([local_mean, local_square, jnp.full((channels,), local_count)])
    )
    width = channels // down
    source = lax.broadcasted_iota(I32, (8 * channels, 1), 0)
    spot = lax.broadcasted_iota(I32, (1, down * channels), 1)
    order = (
        source == (spot // width) % 8 * channels + spot // channels * width + spot % width
    ).astype(BF16)
    conv_part = product(cols, conv_out, extra=16)
    stats, place_rows, conv_part, order = lax.optimization_barrier(
        (stats, place_rows, conv_part, order)
    )
    counts = stats[:, 2]
    total_count = jnp.sum(counts, axis=0)
    center = jnp.sum(stats[:, 0] * counts, axis=0) / total_count
    apart = stats[:, 0] - center
    variance = jnp.sum(stats[:, 1] + counts * apart * apart, axis=0) / total_count
    inverse_std = lax.rsqrt(variance + epsilon)
    normalized = (conv_float - center) * inverse_std
    before = gain * normalized + shift
    activated = (jnp.maximum(before, 0.0) * live_mask).astype(BF16)
    upstream = cotangent[0, 0].astype(F32) * (before > 0.0) * live_mask
    sums = everyones(
        jnp.stack([jnp.sum(upstream, axis=0), jnp.sum(upstream * normalized, axis=0)])
    )
    upstream = upstream.astype(BF16)
    up_part = product(cols, upstream)
    scale = gain * inverse_std
    batch = jnp.stack(
        [scale, inverse_std, center, jnp.broadcast_to(total_count, scale.shape)]
        + [jnp.zeros_like(scale)] * 4
    )
    sums, up_part, batch = lax.optimization_barrier((sums, up_part, batch))
    pieces, conv_grad = weight_terms(
        live_count, sums, batch, upstream, conv_out, up_part, conv_part, order, across, down
    )
    arrived = lax.all_to_all(pieces, axes, 0, 0, tiled=True)
    own_table, *halo = backward(place_rows, place_down, conv_grad, weight, size)
    a0, a2, b0, b2, arrived = from_neighbours(*halo, arrived)
    own_grad = add_back(send_rows[0, 0], a0, a2, b0, b2, own_table)
    summed = jnp.sum(arrived.astype(F32), axis=0).reshape(-1, down, 8, width)
    grad_weight = summed.transpose(0, 2, 1, 3).reshape(-1, down, width)[:TAPS] / jnp.sqrt(
        total_count[0]
    )
    return (activated[None, None], own_grad[None, None], grad_weight)


def solution(mesh):
    return jax.shard_map(
        per_device,
        mesh=mesh,
        in_specs=(
            P("bx", "by", None, None),
            P("bx", "by"),
            P("bx", "by", None, None),
            P("bx", "by", None, None),
            P(),
            P(),
            P(),
            P("bx", "by", None, None),
        ),
        out_specs=(P("bx", "by", None, None), P("bx", "by", None, None), P(None, "bx", "by")),
        check_vma=False,
    )
```

```python
import functools

import jax
import jax.numpy as jnp
from jax import lax
from jax.experimental import pallas as pl
from jax.experimental.pallas import tpu as pltpu
from jax.sharding import PartitionSpec as P

epsilon = 1e-05
axes = ("bx", "by")
F32, BF16, I32 = jnp.float32, jnp.bfloat16, jnp.int32
TAPS = 27


def forward_kernel(chunks, place_ref, own_ref, a0_ref, a2_ref, b0_ref, b2_ref, weight_ref, conv_ref, out_ref, win_ref, cols_ref, sems):
    rows, channels = own_ref.shape
    block = win_ref.shape[0]
    part = block // 8
    high = a0_ref.shape[0] // 3
    wide = TAPS // chunks * channels
    lanes = lax.broadcasted_iota(I32, (block, block), 1)

    def copy_out(q, c):
        return pltpu.make_async_copy(
            cols_ref.at[q, :, pl.ds(c * wide, wide)],
            out_ref.at[pl.ds(q * block, block), pl.ds(c * wide, wide)],
            sems.at[q, c],
        )

    def block_step(q, _):
        here = pl.ds(pl.multiple_of(q * block, block), block)
        win_ref[:, :channels] = own_ref[here, :]
        pieces = (
            (b0_ref, 0), (a0_ref, 1), (b2_ref, 0), (b0_ref, 1),
            (b2_ref, 1), (b0_ref, 2), (a2_ref, 1), (b2_ref, 2),
        )
        for slot, (ref, at) in enumerate(pieces):
            win_ref[pl.ds(slot * part, part), channels:] = ref[
                pl.ds(pl.multiple_of(at * high + q * part, part), part), :
            ]
        place = place_ref[here, :]
        for k in range(TAPS):
            column = jnp.broadcast_to(place[:, k : k + 1], (block, channels))
            beyond = column >= block
            inside = jnp.where(beyond, column - block, column)
            hot = jnp.concatenate(
                [
                    jnp.where(inside == lanes[:, c : c + channels], 1.0, 0.0).astype(BF16)
                    for c in range(0, block, channels)
                ],
                axis=1,
            )
            both = jnp.dot(hot, win_ref[...], preferred_element_type=F32)
            cols_ref[q, :, k * channels : (k + 1) * channels] = jnp.where(
                beyond, both[:, channels:], both[:, :channels]
            ).astype(BF16)
            if (k + 1) % (TAPS // chunks) == 0:
                copy_out(q, k // (TAPS // chunks)).start()
        conv_ref[here, :] = jnp.dot(
            cols_ref[q], weight_ref[...], preferred_element_type=F32
        ).astype(BF16)
        return 0

    lax.fori_loop(0, rows // block, block_step, 0)
    for q in range(rows // block):
        for c in range(chunks):
            copy_out(q, c).wait()


def forward(place, own, a0, a2, b0, b2, weight, block=512, chunks=3):
    rows, channels = own.shape
    vmem = pl.BlockSpec(memory_space=pltpu.VMEM)
    return pl.pallas_call(
        functools.partial(forward_kernel, chunks),
        in_specs=[vmem] * 7,
        out_specs=(vmem, pl.BlockSpec(memory_space=pltpu.HBM)),
        out_shape=(
            jax.ShapeDtypeStruct((rows, channels), BF16),
            pltpu.HBM((rows, TAPS * channels), BF16),
        ),
        scratch_shapes=[
            pltpu.VMEM((block, 2 * channels), BF16),
            pltpu.VMEM((rows // block, block, TAPS * channels), BF16),
            pltpu.SemaphoreType.DMA((rows // block, chunks)),
        ],
        compiler_params=pltpu.CompilerParams(vmem_limit_bytes=20 << 20),
        cost_estimate=pl.CostEstimate(
            flops=TAPS * 4 * rows * channels * block, bytes_accessed=9 << 20, transcendentals=0
        ),
    )(place, own, a0, a2, b0, b2, weight)


def backward_kernel(group, row_ref, place_ref, grad_in_ref, weight_in_ref, own_ref, lo_ref, m0_ref, m2_ref, hi_ref, acc_ref, hot_ref, rhs_ref, grad_ref, weight_ref, sems):
    copies = (
        pltpu.make_async_copy(grad_in_ref, grad_ref, sems.at[0]),
        pltpu.make_async_copy(weight_in_ref, weight_ref, sems.at[1]),
    )
    for copy in copies:
        copy.start()
    for copy in copies:
        copy.wait()
    rows, channels = grad_ref.shape
    block = acc_ref.shape[0]
    part = block // 8
    high = m0_ref.shape[0]
    for q in range(rows // block):
        grad = grad_ref[pl.ds(q * block, block), :]
        place = place_ref[pl.ds(q * block, block), :]
        down = lax.broadcasted_iota(I32, (block, block), 0)
        for g in range(TAPS // group):
            for n in range(group):
                k = g * group + n
                line = row_ref[q, k : k + 1, :]
                line = jnp.where(line >= block, line - block, line)
                hot_ref[:, n * block : (n + 1) * block] = jnp.where(
                    jnp.broadcast_to(line, (block, block)) == down, 1.0, 0.0
                ).astype(BF16)
                back = lax.dot_general(
                    grad, weight_ref[k * channels : (k + 1) * channels, :],
                    (((1,), (1,)), ((), ())), preferred_element_type=F32,
                )
                beyond = jnp.broadcast_to(place[:, k : k + 1], (block, channels)) >= block
                rhs_ref[n * block : (n + 1) * block, :channels] = jnp.where(beyond, 0.0, back).astype(BF16)
                rhs_ref[n * block : (n + 1) * block, channels:] = jnp.where(beyond, back, 0.0).astype(BF16)
            term = jnp.dot(hot_ref[...], rhs_ref[...], preferred_element_type=F32)
            if g == 0:
                acc_ref[...] = term
            else:
                acc_ref[...] += term
        own_ref[pl.ds(q * block, block), :] = acc_ref[:, :channels]
        pieces = (
            (lo_ref, 0), (lo_ref, 1), (lo_ref, 2), (m0_ref, 0),
            (m2_ref, 0), (hi_ref, 0), (hi_ref, 1), (hi_ref, 2),
        )
        for slot, (ref, at) in enumerate(pieces):
            ref[pl.ds(at * high + q * part, part), :] = acc_ref[slot * part : (slot + 1) * part, channels:].astype(BF16)


def backward(row, place, grad, weight, high, block=512, group=3):
    rows, channels = grad.shape
    vmem, hbm = pl.BlockSpec(memory_space=pltpu.VMEM), pl.BlockSpec(memory_space=pltpu.HBM)
    return pl.pallas_call(
        functools.partial(backward_kernel, group),
        in_specs=[vmem, vmem, hbm, hbm],
        out_shape=(
            jax.ShapeDtypeStruct((rows, channels), F32),
            jax.ShapeDtypeStruct((3 * high, channels), BF16),
            jax.ShapeDtypeStruct((high, channels), BF16),
            jax.ShapeDtypeStruct((high, channels), BF16),
            jax.ShapeDtypeStruct((3 * high, channels), BF16),
        ),
        scratch_shapes=[
            pltpu.VMEM((block, 2 * channels), F32),
            pltpu.VMEM((block, group * block), BF16),
            pltpu.VMEM((group * block, 2 * channels), BF16),
            pltpu.VMEM(grad.shape, BF16),
            pltpu.VMEM(weight.shape, BF16),
            pltpu.SemaphoreType.DMA((2,)),
        ],
        compiler_params=pltpu.CompilerParams(vmem_limit_bytes=16 << 20),
        cost_estimate=pl.CostEstimate(flops=TAPS*4*rows*channels*(block+64), bytes_accessed=2<<20, transcendentals=0),
    )(
        row,
        place,
        pltpu.with_memory_space_constraint(grad, pltpu.HBM),
        pltpu.with_memory_space_constraint(weight, pltpu.HBM),
    )


def product_kernel(group, extra, cols_ref, rhs_ref, out_ref, left_ref, whole_ref, buffer_ref, in_sems, out_sems):
    channels = rhs_ref.shape[1]
    wide = group * channels
    slots = buffer_ref.shape[0]
    steps = TAPS // group

    def fetch(step):
        return pltpu.make_async_copy(
            cols_ref.at[:, pl.ds(step * wide, wide)],
            buffer_ref.at[step % slots],
            in_sems.at[step % slots],
        )

    def leave(step):
        here = pl.ds(step * wide, wide)
        return pltpu.make_async_copy(
            whole_ref.at[:, here], out_ref.at[:, here], out_sems.at[step]
        )

    for step in range(slots - 1):
        fetch(step).start()
    left_ref[:channels, :] = rhs_ref[...].T
    if extra:
        left_ref[channels:, :] = jnp.ones((extra, left_ref.shape[1]), BF16)
    for step in range(steps):
        if step + slots - 1 < steps:
            fetch(step + slots - 1).start()
        fetch(step).wait()
        whole_ref[:, step * wide : (step + 1) * wide] = jnp.dot(
            left_ref[...], buffer_ref[step % slots], preferred_element_type=F32
        )
        leave(step).start()
    for step in range(steps):
        leave(step).wait()


def product(cols, rhs, extra=0, group=3, slots=3):
    rows, wide = cols.shape
    channels = rhs.shape[1]
    hbm = pl.BlockSpec(memory_space=pltpu.HBM)
    return pl.pallas_call(
        functools.partial(product_kernel, group, extra),
        in_specs=[hbm, pl.BlockSpec(memory_space=pltpu.VMEM)],
        out_specs=hbm,
        out_shape=pltpu.HBM((channels + extra, wide), F32),
        scratch_shapes=[
            pltpu.VMEM((channels + extra, rows), BF16),
            pltpu.VMEM((channels + extra, wide), F32),
            pltpu.VMEM((slots, rows, group * channels), BF16),
            pltpu.SemaphoreType.DMA((slots,)),
            pltpu.SemaphoreType.DMA((TAPS // group,)),
        ],
        compiler_params=pltpu.CompilerParams(vmem_limit_bytes=16 << 20),
        cost_estimate=pl.CostEstimate(
            flops=2 * rows * wide * channels, bytes_accessed=9 << 20, transcendentals=0
        ),
    )(pltpu.with_memory_space_constraint(cols, pltpu.HBM), rhs)


def weight_kernel(across, down, group, live_ref, sums_ref, batch_ref, upstream_ref, conv_out_ref, up_ref, conv_ref, order_ref, pieces_ref, grad_out_ref, line_ref, first_ref, second_ref, out_ref, grad_ref, sems, out_sems):
    rows, channels = grad_ref.shape
    eighths = pieces_ref.shape[1]
    wide = group * channels
    steps = TAPS // group

    def fetch(step):
        here = pl.ds(step * wide, wide)
        return (
            pltpu.make_async_copy(up_ref.at[:, here], first_ref.at[:, here], sems.at[0, step]),
            pltpu.make_async_copy(conv_ref.at[:, here], second_ref.at[:, here], sems.at[1, step]),
        )

    def line(k):
        return (
            slice(k // 8 * channels, (k // 8 + 1) * channels),
            slice(k % 8 * channels, (k % 8 + 1) * channels),
        )

    for step in range(steps):
        for copy in fetch(step):
            copy.start()
    for k in range(TAPS, 8 * eighths):
        line_ref[line(k)] = jnp.zeros((channels, channels), BF16)
    grad_copy = pltpu.make_async_copy(grad_ref, grad_out_ref, out_sems.at[eighths])
    scale, inverse_std, center, total = [batch_ref[n : n + 1, :] for n in range(4)]
    sums = jnp.sum(sums_ref[...], axis=0)
    mean_up, mean_cross = sums[0:1] / total, sums[1:2] / total
    live = lax.broadcasted_iota(I32, (rows, channels), 0) < live_ref[0, 0]
    normalized = (conv_out_ref[...].astype(F32) - center) * inverse_std
    grad_ref[...] = (
        scale
        * (
            upstream_ref[...].astype(F32)
            - jnp.where(live, mean_up + normalized * mean_cross, 0.0)
        )
    ).astype(BF16)
    grad_copy.start()
    per_cross = scale * mean_cross * inverse_std
    turned = jnp.concatenate(
        [scale, scale * mean_up - per_cross * center, per_cross]
        + [jnp.zeros((5, channels), F32)],
        axis=0,
    ).T
    scales = [jnp.broadcast_to(turned[:, n : n + 1], (channels, channels)) for n in range(3)]
    for step in range(steps):
        for copy in fetch(step):
            copy.wait()
        for k in range(step * group, (step + 1) * group):
            here = slice(k * channels, (k + 1) * channels)
            term = (
                scales[0] * first_ref[:, here]
                - scales[1] * second_ref[channels : channels + 1, here]
                - scales[2] * second_ref[:channels, here]
            )
            line_ref[line(k)] = term.T.astype(BF16)
    placed = jnp.dot(line_ref[...], order_ref[...], preferred_element_type=F32).astype(BF16)
    copies = []
    for e in range(eighths):
        for x in range(across):
            for y in range(down):
                row = e * channels + x * down
                out_ref[x * down + y, e] = placed[
                    row : row + down, y * channels : (y + 1) * channels
                ]
        copies.append(
            pltpu.make_async_copy(out_ref.at[:, e], pieces_ref.at[:, e], out_sems.at[e])
        )
        copies[e].start()
    for copy in copies:
        copy.wait()
    grad_copy.wait()


def weight_terms(live, sums, batch, upstream, conv_out, up_part, conv_part, order, across, down, group=3):
    channels, wide = up_part.shape
    eighths = -(-TAPS // 8)
    vmem, hbm = pl.BlockSpec(memory_space=pltpu.VMEM), pl.BlockSpec(memory_space=pltpu.HBM)
    return pl.pallas_call(
        functools.partial(weight_kernel, across, down, group),
        in_specs=[pl.BlockSpec(memory_space=pltpu.SMEM), vmem, vmem, vmem, vmem, hbm, hbm, vmem],
        out_specs=(hbm, hbm),
        out_shape=(
            pltpu.HBM((across * down, eighths, down, channels), BF16),
            pltpu.HBM(upstream.shape, BF16),
        ),
        scratch_shapes=[
            pltpu.VMEM((eighths * channels, 8 * channels), BF16),
            pltpu.VMEM(up_part.shape, F32),
            pltpu.VMEM(conv_part.shape, F32),
            pltpu.VMEM((across * down, eighths, down, channels), BF16),
            pltpu.VMEM(upstream.shape, BF16),
            pltpu.SemaphoreType.DMA((2, TAPS // group)),
            pltpu.SemaphoreType.DMA((eighths + 1,)),
        ],
        compiler_params=pltpu.CompilerParams(vmem_limit_bytes=20 << 20),
        cost_estimate=pl.CostEstimate(flops=1 << 30, bytes_accessed=5 << 20, transcendentals=0),
    )(
        live,
        sums,
        batch,
        upstream,
        conv_out,
        pltpu.with_memory_space_constraint(up_part, pltpu.HBM),
        pltpu.with_memory_space_constraint(conv_part, pltpu.HBM),
        order,
    )


def add_back_kernel(index_ref, a0_ref, a2_ref, b0_ref, b2_ref, own_ref, out_ref, hot_ref, slot_ref):
    rows, channels = own_ref.shape
    slots, size = index_ref.shape
    down = lax.broadcasted_iota(I32, (rows, size), 0)
    pieces = (
        (b0_ref, 0), (a0_ref, 1), (b2_ref, 0), (b0_ref, 1),
        (b2_ref, 1), (b0_ref, 2), (a2_ref, 1), (b2_ref, 2),
    )
    for slot, (ref, at) in enumerate(pieces):
        slot_ref[slot * size : (slot + 1) * size, :] = ref[at * size : (at + 1) * size, :]
        hot_ref[:, slot * size : (slot + 1) * size] = jnp.where(
            jnp.broadcast_to(index_ref[slot : slot + 1, :], (rows, size)) == down, 1.0, 0.0
        ).astype(BF16)
    added = jnp.dot(hot_ref[...], slot_ref[...], preferred_element_type=F32)
    out_ref[...] = (own_ref[...] + added).astype(BF16)


def add_back(index, a0, a2, b0, b2, own):
    rows, channels = own.shape
    return pl.pallas_call(
        add_back_kernel,
        out_shape=jax.ShapeDtypeStruct((rows, channels), BF16),
        scratch_shapes=[
            pltpu.VMEM((rows, index.size), BF16),
            pltpu.VMEM((index.size, channels), BF16),
        ],
        compiler_params=pltpu.CompilerParams(vmem_limit_bytes=16 << 20),
        cost_estimate=pl.CostEstimate(
            flops=2 * rows * rows * channels, bytes_accessed=2 << 20, transcendentals=0
        ),
    )(index, a0, a2, b0, b2, own)


def from_neighbours(low, mid_low, mid_high, high, arrived):
    size = mid_low.shape[0]
    ends_x, ends_y = lax.axis_size("bx") - 1, lax.axis_size("by") - 1
    up_x, down_x = [(i, i + 1) for i in range(ends_x)], [(i + 1, i) for i in range(ends_x)]
    up_y, down_y = [(i, i + 1) for i in range(ends_y)], [(i + 1, i) for i in range(ends_y)]
    a0 = lax.ppermute(high, "bx", up_x)
    a2 = lax.ppermute(low, "bx", down_x)
    a0, a2, arrived = lax.optimization_barrier((a0, a2, arrived))
    b0 = lax.ppermute(jnp.concatenate([a0[2 * size :], mid_high, a2[2 * size :]]), "by", up_y)
    b2 = lax.ppermute(jnp.concatenate([a0[:size], mid_low, a2[:size]]), "by", down_y)
    return a0, a2, b0, b2, arrived


def everyones(rows):
    devices = lax.axis_size("bx") * lax.axis_size("by")
    copies = jnp.broadcast_to(rows[None], (devices,) + rows.shape)
    return lax.all_to_all(copies, axes, 0, 0, tiled=True)


def per_device(features, live_count, neighbour_map, send_rows, weight, gain, shift, cotangent):
    own_rows = features[0, 0]
    rows_total, channels = own_rows.shape
    size = send_rows.shape[3]
    block_rows = min(rows_total, 512)
    part = size * block_rows // rows_total
    across, down = lax.axis_size("bx"), lax.axis_size("by")
    sent_index = send_rows[0, 0].reshape(-1)
    send_select = (
        sent_index[:, None] == lax.broadcasted_iota(I32, (1, rows_total), 1)
    ).astype(BF16)
    chosen = jnp.dot(send_select, own_rows, preferred_element_type=F32).astype(BF16)
    a0, a2, b0, b2, indices = from_neighbours(
        chosen[: 3 * size],
        chosen[3 * size : 4 * size],
        chosen[4 * size : 5 * size],
        chosen[5 * size :],
        neighbour_map[0, 0],
    )

    block = lax.broadcasted_iota(I32, (1, rows_total), 1) // block_rows
    beyond = indices - rows_total
    target = beyond // size
    inside = beyond - target * size - block * part
    remote = block_rows + (target - (target > 4)) * part + inside
    usable = (inside >= 0) & (inside < part) & (target != 4)
    place = jnp.where(
        indices < rows_total, indices - block * block_rows, jnp.where(usable, remote, -1)
    )
    place = jnp.pad(place, ((0, 5), (0, 0)), constant_values=-1)
    place_down = place.T
    place_rows = place.reshape(-1, rows_total // block_rows, block_rows).transpose(1, 0, 2)

    conv_out, cols = forward(place_down, own_rows, a0, a2, b0, b2, weight)
    conv_float = conv_out.astype(F32)
    live_mask = (lax.broadcasted_iota(I32, (rows_total, 1), 0) < live_count[0, 0]).astype(F32)
    local_count = live_count[0, 0].astype(F32)
    local_mean = jnp.sum(conv_float * live_mask, axis=0) / local_count
    local_dev = (conv_float - local_mean) * live_mask
    local_square = jnp.sum(local_dev * local_dev, axis=0)
    stats = everyones(
        jnp.stack([local_mean, local_square, jnp.full((channels,), local_count)])
    )
    conv_part = product(cols, conv_out, extra=16)
    stats, conv_part = lax.optimization_barrier((stats, conv_part))
    counts = stats[:, 2]
    total_count = jnp.sum(counts, axis=0)
    center = jnp.sum(stats[:, 0] * counts, axis=0) / total_count
    apart = stats[:, 0] - center
    variance = jnp.sum(stats[:, 1] + counts * apart * apart, axis=0) / total_count
    inverse_std = lax.rsqrt(variance + epsilon)
    normalized = (conv_float - center) * inverse_std
    before = gain * normalized + shift
    activated = (jnp.maximum(before, 0.0) * live_mask).astype(BF16)
    upstream = cotangent[0, 0].astype(F32) * (before > 0.0) * live_mask
    sums = everyones(
        jnp.stack([jnp.sum(upstream, axis=0), jnp.sum(upstream * normalized, axis=0)])
    )
    upstream = upstream.astype(BF16)
    up_part = product(cols, upstream)
    scale = gain * inverse_std
    batch = jnp.stack(
        [scale, inverse_std, center, jnp.broadcast_to(total_count, scale.shape)]
        + [jnp.zeros_like(scale)] * 4
    )
    width = channels // down
    source = lax.broadcasted_iota(I32, (8 * channels, 1), 0)
    spot = lax.broadcasted_iota(I32, (1, down * channels), 1)
    order = (
        source == (spot // width) % 8 * channels + spot // channels * width + spot % width
    ).astype(BF16)
    sums, up_part, batch, order = lax.optimization_barrier((sums, up_part, batch, order))
    pieces, conv_grad = weight_terms(
        live_count, sums, batch, upstream, conv_out, up_part, conv_part, order, across, down
    )
    arrived = lax.all_to_all(pieces, axes, 0, 0, tiled=True)
    own_table, *halo = backward(place_rows, place_down, conv_grad, weight, size)
    a0, a2, b0, b2, arrived = from_neighbours(*halo, arrived)
    own_grad = add_back(send_rows[0, 0], a0, a2, b0, b2, own_table)
    summed = jnp.sum(arrived.astype(F32), axis=0).reshape(-1, down, 8, width)
    grad_weight = summed.transpose(0, 2, 1, 3).reshape(-1, down, width)[:TAPS] / jnp.sqrt(
        total_count[0]
    )
    return (activated[None, None], own_grad[None, None], grad_weight)


def solution(mesh):
    return jax.shard_map(
        per_device,
        mesh=mesh,
        in_specs=(
            P("bx", "by", None, None),
            P("bx", "by"),
            P("bx", "by", None, None),
            P("bx", "by", None, None),
            P(),
            P(),
            P(),
            P("bx", "by", None, None),
        ),
        out_specs=(P("bx", "by", None, None), P("bx", "by", None, None), P(None, "bx", "by")),
        check_vma=False,
    )
```

```python
import functools

import jax
import jax.numpy as jnp
from jax import lax
from jax.experimental import pallas as pl
from jax.experimental.pallas import tpu as pltpu
from jax.sharding import PartitionSpec as P

epsilon = 1e-05
axes = ("bx", "by")
F32, BF16, I32 = jnp.float32, jnp.bfloat16, jnp.int32
TAPS = 27


def forward_kernel(chunks, place_ref, own_ref, a0_ref, a2_ref, b0_ref, b2_ref, weight_ref, conv_ref, out_ref, win_ref, cols_ref, sems):
    rows, channels = own_ref.shape
    block = win_ref.shape[0]
    part = block // 8
    high = a0_ref.shape[0] // 3
    wide = TAPS // chunks * channels
    lanes = lax.broadcasted_iota(I32, (block, block), 1)

    def copy_out(q, c):
        return pltpu.make_async_copy(
            cols_ref.at[q, :, pl.ds(c * wide, wide)],
            out_ref.at[pl.ds(q * block, block), pl.ds(c * wide, wide)],
            sems.at[q, c],
        )

    def block_step(q, _):
        here = pl.ds(pl.multiple_of(q * block, block), block)
        win_ref[:, :channels] = own_ref[here, :]
        pieces = (
            (b0_ref, 0), (a0_ref, 1), (b2_ref, 0), (b0_ref, 1),
            (b2_ref, 1), (b0_ref, 2), (a2_ref, 1), (b2_ref, 2),
        )
        for slot, (ref, at) in enumerate(pieces):
            win_ref[pl.ds(slot * part, part), channels:] = ref[
                pl.ds(pl.multiple_of(at * high + q * part, part), part), :
            ]
        place = place_ref[here, :]
        for k in range(TAPS):
            column = jnp.broadcast_to(place[:, k : k + 1], (block, channels))
            beyond = column >= block
            inside = jnp.where(beyond, column - block, column)
            hot = jnp.concatenate(
                [
                    jnp.where(inside == lanes[:, c : c + channels], 1.0, 0.0).astype(BF16)
                    for c in range(0, block, channels)
                ],
                axis=1,
            )
            both = jnp.dot(hot, win_ref[...], preferred_element_type=F32)
            cols_ref[q, :, k * channels : (k + 1) * channels] = jnp.where(
                beyond, both[:, channels:], both[:, :channels]
            ).astype(BF16)
            if (k + 1) % (TAPS // chunks) == 0:
                copy_out(q, k // (TAPS // chunks)).start()
        conv_ref[here, :] = jnp.dot(
            cols_ref[q], weight_ref[...], preferred_element_type=F32
        ).astype(BF16)
        return 0

    lax.fori_loop(0, rows // block, block_step, 0)
    for q in range(rows // block):
        for c in range(chunks):
            copy_out(q, c).wait()


def forward(place, own, a0, a2, b0, b2, weight, block=512, chunks=3):
    rows, channels = own.shape
    vmem = pl.BlockSpec(memory_space=pltpu.VMEM)
    return pl.pallas_call(
        functools.partial(forward_kernel, chunks),
        in_specs=[vmem] * 7,
        out_specs=(vmem, pl.BlockSpec(memory_space=pltpu.HBM)),
        out_shape=(
            jax.ShapeDtypeStruct((rows, channels), BF16),
            pltpu.HBM((rows, TAPS * channels), BF16),
        ),
        scratch_shapes=[
            pltpu.VMEM((block, 2 * channels), BF16),
            pltpu.VMEM((rows // block, block, TAPS * channels), BF16),
            pltpu.SemaphoreType.DMA((rows // block, chunks)),
        ],
        compiler_params=pltpu.CompilerParams(vmem_limit_bytes=20 << 20),
        cost_estimate=pl.CostEstimate(
            flops=TAPS * 4 * rows * channels * block, bytes_accessed=9 << 20, transcendentals=0
        ),
    )(place, own, a0, a2, b0, b2, weight)


def backward_kernel(group, row_ref, place_ref, grad_in_ref, weight_in_ref, own_ref, lo_ref, m0_ref, m2_ref, hi_ref, acc_ref, hot_ref, rhs_ref, grad_ref, weight_ref, sems):
    copies = (
        pltpu.make_async_copy(grad_in_ref, grad_ref, sems.at[0]),
        pltpu.make_async_copy(weight_in_ref, weight_ref, sems.at[1]),
    )
    for copy in copies:
        copy.start()
    for copy in copies:
        copy.wait()
    rows, channels = grad_ref.shape
    block = acc_ref.shape[0]
    part = block // 8
    high = m0_ref.shape[0]
    for q in range(rows // block):
        grad = grad_ref[pl.ds(q * block, block), :]
        place = place_ref[pl.ds(q * block, block), :]
        down = lax.broadcasted_iota(I32, (block, block), 0)
        for g in range(TAPS // group):
            for n in range(group):
                k = g * group + n
                line = row_ref[q, k : k + 1, :]
                line = jnp.where(line >= block, line - block, line)
                hot_ref[:, n * block : (n + 1) * block] = jnp.where(
                    jnp.broadcast_to(line, (block, block)) == down, 1.0, 0.0
                ).astype(BF16)
                back = lax.dot_general(
                    grad, weight_ref[k * channels : (k + 1) * channels, :],
                    (((1,), (1,)), ((), ())), preferred_element_type=F32,
                )
                beyond = jnp.broadcast_to(place[:, k : k + 1], (block, channels)) >= block
                rhs_ref[n * block : (n + 1) * block, :channels] = jnp.where(beyond, 0.0, back).astype(BF16)
                rhs_ref[n * block : (n + 1) * block, channels:] = jnp.where(beyond, back, 0.0).astype(BF16)
            term = jnp.dot(hot_ref[...], rhs_ref[...], preferred_element_type=F32)
            if g == 0:
                acc_ref[...] = term
            else:
                acc_ref[...] += term
        own_ref[pl.ds(q * block, block), :] = acc_ref[:, :channels]
        pieces = (
            (lo_ref, 0), (lo_ref, 1), (lo_ref, 2), (m0_ref, 0),
            (m2_ref, 0), (hi_ref, 0), (hi_ref, 1), (hi_ref, 2),
        )
        for slot, (ref, at) in enumerate(pieces):
            ref[pl.ds(at * high + q * part, part), :] = acc_ref[slot * part : (slot + 1) * part, channels:].astype(BF16)


def backward(row, place, grad, weight, high, block=512, group=3):
    rows, channels = grad.shape
    vmem, hbm = pl.BlockSpec(memory_space=pltpu.VMEM), pl.BlockSpec(memory_space=pltpu.HBM)
    return pl.pallas_call(
        functools.partial(backward_kernel, group),
        in_specs=[vmem, vmem, hbm, hbm],
        out_shape=(
            jax.ShapeDtypeStruct((rows, channels), F32),
            jax.ShapeDtypeStruct((3 * high, channels), BF16),
            jax.ShapeDtypeStruct((high, channels), BF16),
            jax.ShapeDtypeStruct((high, channels), BF16),
            jax.ShapeDtypeStruct((3 * high, channels), BF16),
        ),
        scratch_shapes=[
            pltpu.VMEM((block, 2 * channels), F32),
            pltpu.VMEM((block, group * block), BF16),
            pltpu.VMEM((group * block, 2 * channels), BF16),
            pltpu.VMEM(grad.shape, BF16),
            pltpu.VMEM(weight.shape, BF16),
            pltpu.SemaphoreType.DMA((2,)),
        ],
        compiler_params=pltpu.CompilerParams(vmem_limit_bytes=16 << 20),
        cost_estimate=pl.CostEstimate(flops=TAPS*4*rows*channels*(block+64), bytes_accessed=2<<20, transcendentals=0),
    )(
        row,
        place,
        pltpu.with_memory_space_constraint(grad, pltpu.HBM),
        pltpu.with_memory_space_constraint(weight, pltpu.HBM),
    )


def product_kernel(group, extra, cols_ref, rhs_ref, out_ref, left_ref, whole_ref, buffer_ref, in_sems, out_sems):
    channels = rhs_ref.shape[1]
    wide = group * channels
    slots = buffer_ref.shape[0]
    steps = TAPS // group

    def fetch(step):
        return pltpu.make_async_copy(
            cols_ref.at[:, pl.ds(step * wide, wide)],
            buffer_ref.at[step % slots],
            in_sems.at[step % slots],
        )

    def leave(step):
        here = pl.ds(step * wide, wide)
        return pltpu.make_async_copy(
            whole_ref.at[:, here], out_ref.at[:, here], out_sems.at[step]
        )

    for step in range(slots - 1):
        fetch(step).start()
    left_ref[:channels, :] = rhs_ref[...].T
    if extra:
        left_ref[channels:, :] = jnp.ones((extra, left_ref.shape[1]), BF16)
    for step in range(steps):
        if step + slots - 1 < steps:
            fetch(step + slots - 1).start()
        fetch(step).wait()
        whole_ref[:, step * wide : (step + 1) * wide] = jnp.dot(
            left_ref[...], buffer_ref[step % slots], preferred_element_type=F32
        )
        leave(step).start()
    for step in range(steps):
        leave(step).wait()


def product(cols, rhs, extra=0, group=3, slots=3):
    rows, wide = cols.shape
    channels = rhs.shape[1]
    hbm = pl.BlockSpec(memory_space=pltpu.HBM)
    return pl.pallas_call(
        functools.partial(product_kernel, group, extra),
        in_specs=[hbm, pl.BlockSpec(memory_space=pltpu.VMEM)],
        out_specs=hbm,
        out_shape=pltpu.HBM((channels + extra, wide), F32),
        scratch_shapes=[
            pltpu.VMEM((channels + extra, rows), BF16),
            pltpu.VMEM((channels + extra, wide), F32),
            pltpu.VMEM((slots, rows, group * channels), BF16),
            pltpu.SemaphoreType.DMA((slots,)),
            pltpu.SemaphoreType.DMA((TAPS // group,)),
        ],
        compiler_params=pltpu.CompilerParams(vmem_limit_bytes=8 << 20),
        cost_estimate=pl.CostEstimate(
            flops=2 * rows * wide * channels, bytes_accessed=9 << 20, transcendentals=0
        ),
    )(pltpu.with_memory_space_constraint(cols, pltpu.HBM), rhs)


def weight_kernel(across, down, group, live_ref, sums_ref, batch_ref, upstream_ref, conv_out_ref, up_ref, conv_ref, order_ref, pieces_ref, grad_out_ref, line_ref, first_ref, second_ref, out_ref, grad_ref, sems, out_sems):
    rows, channels = grad_ref.shape
    eighths = pieces_ref.shape[1]
    wide = group * channels
    steps = TAPS // group

    def fetch(step):
        here = pl.ds(step * wide, wide)
        return (
            pltpu.make_async_copy(up_ref.at[:, here], first_ref.at[:, here], sems.at[0, step]),
            pltpu.make_async_copy(conv_ref.at[:, here], second_ref.at[:, here], sems.at[1, step]),
        )

    def line(k):
        return (
            slice(k // 8 * channels, (k // 8 + 1) * channels),
            slice(k % 8 * channels, (k % 8 + 1) * channels),
        )

    for step in range(steps):
        for copy in fetch(step):
            copy.start()
    for k in range(TAPS, 8 * eighths):
        line_ref[line(k)] = jnp.zeros((channels, channels), BF16)
    grad_copy = pltpu.make_async_copy(grad_ref, grad_out_ref, out_sems.at[eighths])
    scale, inverse_std, center, total = [batch_ref[n : n + 1, :] for n in range(4)]
    sums = jnp.sum(sums_ref[...], axis=0)
    mean_up, mean_cross = sums[0:1] / total, sums[1:2] / total
    live = lax.broadcasted_iota(I32, (rows, channels), 0) < live_ref[0, 0]
    normalized = (conv_out_ref[...].astype(F32) - center) * inverse_std
    grad_ref[...] = (
        scale
        * (
            upstream_ref[...].astype(F32)
            - jnp.where(live, mean_up + normalized * mean_cross, 0.0)
        )
    ).astype(BF16)
    grad_copy.start()
    per_cross = scale * mean_cross * inverse_std
    turned = jnp.concatenate(
        [scale, scale * mean_up - per_cross * center, per_cross]
        + [jnp.zeros((5, channels), F32)],
        axis=0,
    ).T
    scales = [jnp.broadcast_to(turned[:, n : n + 1], (channels, channels)) for n in range(3)]
    for step in range(steps):
        for copy in fetch(step):
            copy.wait()
        for k in range(step * group, (step + 1) * group):
            here = slice(k * channels, (k + 1) * channels)
            term = (
                scales[0] * first_ref[:, here]
                - scales[1] * second_ref[channels : channels + 1, here]
                - scales[2] * second_ref[:channels, here]
            )
            line_ref[line(k)] = term.T.astype(BF16)
    placed = jnp.dot(line_ref[...], order_ref[...], preferred_element_type=F32).astype(BF16)
    copies = []
    for e in range(eighths):
        for x in range(across):
            for y in range(down):
                row = e * channels + x * down
                out_ref[x * down + y, e] = placed[
                    row : row + down, y * channels : (y + 1) * channels
                ]
        copies.append(
            pltpu.make_async_copy(out_ref.at[:, e], pieces_ref.at[:, e], out_sems.at[e])
        )
        copies[e].start()
    for copy in copies:
        copy.wait()
    grad_copy.wait()


def weight_terms(live, sums, batch, upstream, conv_out, up_part, conv_part, order, across, down, group=3):
    channels, wide = up_part.shape
    eighths = -(-TAPS // 8)
    vmem, hbm = pl.BlockSpec(memory_space=pltpu.VMEM), pl.BlockSpec(memory_space=pltpu.HBM)
    return pl.pallas_call(
        functools.partial(weight_kernel, across, down, group),
        in_specs=[pl.BlockSpec(memory_space=pltpu.SMEM), vmem, vmem, vmem, vmem, hbm, hbm, vmem],
        out_specs=(hbm, hbm),
        out_shape=(
            pltpu.HBM((across * down, eighths, down, channels), BF16),
            pltpu.HBM(upstream.shape, BF16),
        ),
        scratch_shapes=[
            pltpu.VMEM((eighths * channels, 8 * channels), BF16),
            pltpu.VMEM(up_part.shape, F32),
            pltpu.VMEM(conv_part.shape, F32),
            pltpu.VMEM((across * down, eighths, down, channels), BF16),
            pltpu.VMEM(upstream.shape, BF16),
            pltpu.SemaphoreType.DMA((2, TAPS // group)),
            pltpu.SemaphoreType.DMA((eighths + 1,)),
        ],
        compiler_params=pltpu.CompilerParams(vmem_limit_bytes=20 << 20),
        cost_estimate=pl.CostEstimate(flops=1 << 30, bytes_accessed=5 << 20, transcendentals=0),
    )(
        live,
        sums,
        batch,
        upstream,
        conv_out,
        pltpu.with_memory_space_constraint(up_part, pltpu.HBM),
        pltpu.with_memory_space_constraint(conv_part, pltpu.HBM),
        order,
    )


def add_back_kernel(index_ref, a0_ref, a2_ref, b0_ref, b2_ref, own_ref, out_ref, hot_ref, slot_ref):
    rows, channels = own_ref.shape
    slots, size = index_ref.shape
    down = lax.broadcasted_iota(I32, (rows, size), 0)
    pieces = (
        (b0_ref, 0), (a0_ref, 1), (b2_ref, 0), (b0_ref, 1),
        (b2_ref, 1), (b0_ref, 2), (a2_ref, 1), (b2_ref, 2),
    )
    for slot, (ref, at) in enumerate(pieces):
        slot_ref[slot * size : (slot + 1) * size, :] = ref[at * size : (at + 1) * size, :]
        hot_ref[:, slot * size : (slot + 1) * size] = jnp.where(
            jnp.broadcast_to(index_ref[slot : slot + 1, :], (rows, size)) == down, 1.0, 0.0
        ).astype(BF16)
    added = jnp.dot(hot_ref[...], slot_ref[...], preferred_element_type=F32)
    out_ref[...] = (own_ref[...] + added).astype(BF16)


def add_back(index, a0, a2, b0, b2, own):
    rows, channels = own.shape
    return pl.pallas_call(
        add_back_kernel,
        out_shape=jax.ShapeDtypeStruct((rows, channels), BF16),
        scratch_shapes=[
            pltpu.VMEM((rows, index.size), BF16),
            pltpu.VMEM((index.size, channels), BF16),
        ],
        compiler_params=pltpu.CompilerParams(vmem_limit_bytes=16 << 20),
        cost_estimate=pl.CostEstimate(
            flops=2 * rows * rows * channels, bytes_accessed=2 << 20, transcendentals=0
        ),
    )(index, a0, a2, b0, b2, own)


def from_neighbours(low, mid_low, mid_high, high, arrived):
    size = mid_low.shape[0]
    ends_x, ends_y = lax.axis_size("bx") - 1, lax.axis_size("by") - 1
    up_x, down_x = [(i, i + 1) for i in range(ends_x)], [(i + 1, i) for i in range(ends_x)]
    up_y, down_y = [(i, i + 1) for i in range(ends_y)], [(i + 1, i) for i in range(ends_y)]
    a0 = lax.ppermute(high, "bx", up_x)
    a2 = lax.ppermute(low, "bx", down_x)
    a0, a2, arrived = lax.optimization_barrier((a0, a2, arrived))
    b0 = lax.ppermute(jnp.concatenate([a0[2 * size :], mid_high, a2[2 * size :]]), "by", up_y)
    b2 = lax.ppermute(jnp.concatenate([a0[:size], mid_low, a2[:size]]), "by", down_y)
    return a0, a2, b0, b2, arrived


def everyones(rows):
    devices = lax.axis_size("bx") * lax.axis_size("by")
    copies = jnp.broadcast_to(rows[None], (devices,) + rows.shape)
    return lax.all_to_all(copies, axes, 0, 0, tiled=True)


def per_device(features, live_count, neighbour_map, send_rows, weight, gain, shift, cotangent):
    own_rows = features[0, 0]
    rows_total, channels = own_rows.shape
    size = send_rows.shape[3]
    block_rows = min(rows_total, 512)
    part = size * block_rows // rows_total
    across, down = lax.axis_size("bx"), lax.axis_size("by")
    sent_index = send_rows[0, 0].reshape(-1)
    send_select = (
        sent_index[:, None] == lax.broadcasted_iota(I32, (1, rows_total), 1)
    ).astype(BF16)
    chosen = jnp.dot(send_select, own_rows, preferred_element_type=F32).astype(BF16)
    a0, a2, b0, b2, indices = from_neighbours(
        chosen[: 3 * size],
        chosen[3 * size : 4 * size],
        chosen[4 * size : 5 * size],
        chosen[5 * size :],
        neighbour_map[0, 0],
    )

    block = lax.broadcasted_iota(I32, (1, rows_total), 1) // block_rows
    beyond = indices - rows_total
    target = beyond // size
    inside = beyond - target * size - block * part
    remote = block_rows + (target - (target > 4)) * part + inside
    usable = (inside >= 0) & (inside < part) & (target != 4)
    place = jnp.where(
        indices < rows_total, indices - block * block_rows, jnp.where(usable, remote, -1)
    )
    place = jnp.pad(place, ((0, 5), (0, 0)), constant_values=-1)
    place_down = place.T
    place_rows = place.reshape(-1, rows_total // block_rows, block_rows).transpose(1, 0, 2)

    conv_out, cols = forward(place_down, own_rows, a0, a2, b0, b2, weight)
    conv_float = conv_out.astype(F32)
    live_mask = (lax.broadcasted_iota(I32, (rows_total, 1), 0) < live_count[0, 0]).astype(F32)
    local_count = live_count[0, 0].astype(F32)
    local_mean = jnp.sum(conv_float * live_mask, axis=0) / local_count
    local_dev = (conv_float - local_mean) * live_mask
    local_square = jnp.sum(local_dev * local_dev, axis=0)
    stats = everyones(
        jnp.stack([local_mean, local_square, jnp.full((channels,), local_count)])
    )
    conv_part = product(cols, conv_out, extra=16)
    stats, conv_part = lax.optimization_barrier((stats, conv_part))
    counts = stats[:, 2]
    total_count = jnp.sum(counts, axis=0)
    center = jnp.sum(stats[:, 0] * counts, axis=0) / total_count
    apart = stats[:, 0] - center
    variance = jnp.sum(stats[:, 1] + counts * apart * apart, axis=0) / total_count
    inverse_std = lax.rsqrt(variance + epsilon)
    normalized = (conv_float - center) * inverse_std
    before = gain * normalized + shift
    activated = (jnp.maximum(before, 0.0) * live_mask).astype(BF16)
    upstream = cotangent[0, 0].astype(F32) * (before > 0.0) * live_mask
    sums = everyones(
        jnp.stack([jnp.sum(upstream, axis=0), jnp.sum(upstream * normalized, axis=0)])
    )
    upstream = upstream.astype(BF16)
    up_part = product(cols, upstream)
    scale = gain * inverse_std
    batch = jnp.stack(
        [scale, inverse_std, center, jnp.broadcast_to(total_count, scale.shape)]
        + [jnp.zeros_like(scale)] * 4
    )
    width = channels // down
    source = lax.broadcasted_iota(I32, (8 * channels, 1), 0)
    spot = lax.broadcasted_iota(I32, (1, down * channels), 1)
    order = (
        source == (spot // width) % 8 * channels + spot // channels * width + spot % width
    ).astype(BF16)
    sums, up_part, batch, order, place_rows = lax.optimization_barrier(
        (sums, up_part, batch, order, place_rows)
    )
    pieces, conv_grad = weight_terms(
        live_count, sums, batch, upstream, conv_out, up_part, conv_part, order, across, down
    )
    arrived = lax.all_to_all(pieces, axes, 0, 0, tiled=True)
    own_table, *halo = backward(place_rows, place_down, conv_grad, weight, size)
    a0, a2, b0, b2, arrived = from_neighbours(*halo, arrived)
    own_grad = add_back(send_rows[0, 0], a0, a2, b0, b2, own_table)
    summed = jnp.sum(arrived.astype(F32), axis=0).reshape(-1, down, 8, width)
    grad_weight = summed.transpose(0, 2, 1, 3).reshape(-1, down, width)[:TAPS] / jnp.sqrt(
        total_count[0]
    )
    return (activated[None, None], own_grad[None, None], grad_weight)


def solution(mesh):
    return jax.shard_map(
        per_device,
        mesh=mesh,
        in_specs=(
            P("bx", "by", None, None),
            P("bx", "by"),
            P("bx", "by", None, None),
            P("bx", "by", None, None),
            P(),
            P(),
            P(),
            P("bx", "by", None, None),
        ),
        out_specs=(P("bx", "by", None, None), P("bx", "by", None, None), P(None, "bx", "by")),
        check_vma=False,
    )
```
